32 devices in a mesh: dp: 2 (over x), seq: 16 (over z, y, core).
Axes of the slice: x: 2, y: 2, z: 4, core: 2. Of those that a mesh axis runs over, the one named last changes fastest.
Arguments:
- hidden_in: bfloat16 [2, 3072, 3584], P('dp', 'seq'), may hold values from -6 to 6
- spike_level: int32 [2, 3072], P('dp', 'seq'), may hold values from 1 to 4
- value_weight: bfloat16 [3584, 256], P('dp'), may hold values from -0.09375 to 0.09375
- queries: bfloat16 [2, 3072, 1792], P('dp', 'seq'), may hold values from -32 to 32
- key_states: bfloat16 [2, 3072, 256], P('dp', 'seq'), may hold values from -32 to 32
- spike_mask: int32 [2, 3072, 14], P('dp', 'seq'), may hold values 0 or 1
- out_grad: bfloat16 [2, 3072, 1792], P('dp', 'seq'), may hold values from -6 to 6
Outputs:
- query_grad: bfloat16 [2, 3072, 1792], P('dp', 'seq')
- key_grad: bfloat16 [2, 3072, 256], P('dp', 'seq')
- value_weight_grad: bfloat16 [3584, 256], P('dp')
The draws below stay inside these ranges and needn't reach their ends.
All inputs are finite; a program needn't handle non-finite values. No bound on the sum of `spike_mask` on one device may be relied on, other than what follows from the above.
Results may differ from the reference program's by a relative error of at most 0.012.
The reference program's roundings to bfloat16 on the way count: a program that leaves them out, or rounds other values in their place, can miss the bound.
Values may be sent and summed in bfloat16 or wider, within the bound.
No kernel may reach another device: no remote copies, remote signals or barrier semaphores. Data moves between devices by JAX's collectives and lax.ppermute only.
A program may use at most 64 MiB of HBM per device.

```python
import math
import jax
import jax.numpy as jnp
from jax import lax

D = 3584
QH = 14
KVH = 2
HD = 128
WINDOW = 512
LEVELS = 4
TOK_DEV = 192
GROUP = 7
REACH = 3
SEQLEN = 3072
SEQS = 2
N_SEQ = 16


def drawn_rows(key):
    base = jnp.clip(jax.random.normal(jax.random.fold_in(key, 7), (SEQS, SEQLEN, KVH, HD), jnp.float32), -5.0, 5.0)
    return base


def draw_key_states(key, part):
    base = drawn_rows(key)
    states = base
    return states.reshape(SEQS, SEQLEN, KVH * HD).astype(jnp.bfloat16)


def draw_queries(key, part):
    noise = jnp.clip(jax.random.normal(jax.random.fold_in(key, 10), (SEQS, SEQLEN, QH, HD), jnp.float32), -5.0, 5.0)
    return noise.reshape(SEQS, SEQLEN, QH * HD).astype(jnp.bfloat16)


def set_ends(array, stream_key, low, top_value):
    shape = array.shape
    index_at = [jax.random.randint(jax.random.fold_in(stream_key, axis), (), 0, shape[axis]) for axis in range(len(shape))]
    array = array.at[tuple(index_at)].set(low)
    longest = shape.index(max(shape))
    index_at[longest] = (index_at[longest] + 1) % shape[longest]
    return array.at[tuple(index_at)].set(top_value)


def with_spikes(array, own_key, source, target, parts, factor):
    owner, partner = [(jnp.arange(array.shape[position]) // (array.shape[position] // parts)).reshape([-1 if axis == position else 1 for axis in range(array.ndim)]) for position in (source, target)]
    chosen = jax.random.permutation(own_key, parts)[partner]
    strong = (owner == chosen) | (owner == (partner + parts // 2) % parts)
    return jnp.where(strong, factor * array, array)


def shard_levels(stream_key, dims, pieces, smallest, largest):
    loudness, own = 1.0, jax.random.fold_in(stream_key, 6)
    for position, parts in pieces:
        steps = jnp.exp(jax.random.uniform(jax.random.fold_in(own, position), (parts,), jnp.float32, smallest / len(pieces), largest / len(pieces)))
        loudness = loudness * jnp.repeat(steps, dims[position] // parts).reshape([-1 if axis == position else 1 for axis in range(len(dims))])
    return loudness


def normal_values(key, extent, deviation, limit, shards=(), kind=jnp.bfloat16):
    drawn = jax.random.normal(key, extent, jnp.float32) * deviation
    if len(shards) > 0:
        drawn = shard_levels(key, extent, shards, -0.22, 0.18) * drawn
    return jnp.clip(drawn, min=-limit, max=limit).astype(kind)


def bell_draw_with(own_key, dims, spread, reach, split, heavy, kind=jnp.bfloat16):
    entries = spread * jax.random.normal(own_key, dims, jnp.float32)
    if split:
        entries = entries * shard_levels(own_key, dims, split, -0.22, 0.18)
    return jnp.clip(with_spikes(entries, jax.random.fold_in(own_key, 3), *heavy), -reach, reach).astype(kind)


def setup_inputs(seed: int = 0) -> dict:
    key_of = jax.random.split(jax.random.key(seed), 8)
    return {
        "hidden_in": bell_draw_with(key_of[0], (SEQS, SEQLEN, D), 1.0, 6.0, ((0, 2), (1, 16)), (1, 2, 16, 2.0)),
        "spike_level": set_ends(jax.random.randint(key_of[1], (SEQS, SEQLEN), 1, 5), jax.random.fold_in(key_of[1], 1), 1, 4).astype(jnp.int32),
        "value_weight": normal_values(key_of[2], (D, KVH * HD), D ** -0.5, 0.09375, ((0, 2),)),
        "queries": draw_queries(jax.random.fold_in(key_of[7], 71), 0),
        "key_states": draw_key_states(jax.random.fold_in(key_of[7], 71), 0),
        "spike_mask": set_ends((jax.random.randint(key_of[5], (SEQS, SEQLEN, QH), 0, 4) < 3).astype(jnp.int32), jax.random.fold_in(key_of[5], 1), 0, 1),
        "out_grad": normal_values(key_of[6], (SEQS, SEQLEN, QH * HD), 1.0, 6.0, ((0, 2), (1, 16))),
    }


masked_score = -1e+30

def reference(hidden_in, spike_level, value_weight, queries, key_states, spike_mask, out_grad):
    score_scale = 1.0 / math.sqrt(HD)
    padding = REACH * TOK_DEV
    key_span = (REACH + 1) * TOK_DEV

    def one_sequence(grad_sum, inputs):
        hidden_seq, level_seq, query_seq, key_seq, grad_seq, mask_seq = inputs
        spiked = (hidden_seq.astype(jnp.float32) * (level_seq.astype(jnp.float32) / LEVELS)[:, None]).astype(jnp.bfloat16)
        values = jnp.dot(spiked, value_weight, preferred_element_type=jnp.float32).astype(jnp.bfloat16)
        keys_padded = jnp.concatenate([jnp.zeros((padding, KVH * HD), jnp.bfloat16), key_seq], axis=0)
        values_padded = jnp.concatenate([jnp.zeros((padding, KVH * HD), jnp.bfloat16), values], axis=0)
        gated = (grad_seq.reshape(SEQLEN, QH, HD) * mask_seq[:, :, None].astype(jnp.bfloat16)).reshape(SEQLEN, QH * HD)

        def block_step(accums, block_index):
            key_acc, value_acc = accums
            begin_row = (block_index * TOK_DEV).astype(jnp.int32)
            query_blk = lax.dynamic_slice_in_dim(query_seq, begin_row, TOK_DEV, 0).reshape(TOK_DEV, KVH, GROUP, HD).astype(jnp.float32)
            gated_blk = lax.dynamic_slice_in_dim(gated, begin_row, TOK_DEV, 0).reshape(TOK_DEV, KVH, GROUP, HD).astype(jnp.float32)
            key_blk = lax.dynamic_slice_in_dim(keys_padded, begin_row, key_span, 0).reshape(key_span, KVH, HD).astype(jnp.float32)
            value_blk = lax.dynamic_slice_in_dim(values_padded, begin_row, key_span, 0).reshape(key_span, KVH, HD).astype(jnp.float32)
            query_pos = begin_row + jnp.arange(TOK_DEV, dtype=jnp.int32)
            key_pos = begin_row - padding + jnp.arange(key_span, dtype=jnp.int32)
            allowed = (key_pos[None, :] <= query_pos[:, None]) & (key_pos[None, :] > query_pos[:, None] - WINDOW) & (key_pos[None, :] >= 0)
            scores = jnp.einsum('tghd,jgd->ghtj', query_blk, key_blk) * score_scale
            scores = jnp.where(allowed[None, None], scores, masked_score)
            highest = lax.optimization_barrier(jnp.max(scores, axis=-1, keepdims=True))
            expo = jnp.exp(scores - highest)
            probs = expo / lax.optimization_barrier(jnp.sum(expo, axis=-1, keepdims=True))
            rounded_probs = lax.optimization_barrier(probs.astype(jnp.bfloat16)).astype(jnp.float32)
            attended = jnp.einsum('ghtj,jgd->tghd', rounded_probs, value_blk)
            delta = lax.optimization_barrier(jnp.sum(gated_blk * attended, axis=-1))
            prob_grad = jnp.einsum('tghd,jgd->ghtj', gated_blk, value_blk)
            score_grad = probs * (prob_grad - jnp.transpose(delta, (1, 2, 0))[..., None])
            score_grad = lax.optimization_barrier(score_grad.astype(jnp.bfloat16)).astype(jnp.float32)
            query_part = (jnp.einsum('ghtj,jgd->tghd', score_grad, key_blk) * score_scale).astype(jnp.bfloat16)
            key_part = jnp.einsum('ghtj,tghd->jgd', score_grad, query_blk) * score_scale
            value_part = jnp.einsum('ghtj,tghd->jgd', rounded_probs, gated_blk)
            old_keys = lax.dynamic_slice_in_dim(key_acc, begin_row, key_span, 0)
            old_values = lax.dynamic_slice_in_dim(value_acc, begin_row, key_span, 0)
            key_acc = lax.dynamic_update_slice_in_dim(key_acc, old_keys + key_part.reshape(key_span, KVH * HD), begin_row, 0)
            value_acc = lax.dynamic_update_slice_in_dim(value_acc, old_values + value_part.reshape(key_span, KVH * HD), begin_row, 0)
            return ((key_acc, value_acc), query_part.reshape(TOK_DEV, QH * HD))
        start_accums = (jnp.zeros((padding + SEQLEN, KVH * HD), jnp.float32), jnp.zeros((padding + SEQLEN, KVH * HD), jnp.float32))
        (key_acc, value_acc), query_parts = lax.scan(block_step, start_accums, jnp.arange(N_SEQ, dtype=jnp.int32))
        key_grad_seq = key_acc[padding:].astype(jnp.bfloat16)
        value_grad_seq = value_acc[padding:].astype(jnp.bfloat16)
        grad_sum = grad_sum + jnp.dot(spiked.T, value_grad_seq, preferred_element_type=jnp.float32)
        return (grad_sum, (query_parts.reshape(SEQLEN, QH * HD), key_grad_seq))
    grad_total, (query_grad, key_grad) = lax.scan(one_sequence, jnp.zeros((D, KVH * HD), jnp.float32), (hidden_in, spike_level, queries, key_states, out_grad, spike_mask))
    return (query_grad, key_grad, grad_total.astype(jnp.bfloat16))
```

```python
import math

import jax
import jax.numpy as jnp
from jax import lax
from jax.sharding import PartitionSpec as P

QH = 14
KVH = 2
HD = 128
WINDOW = 512
LEVELS = 4
GROUP = 7


masked_score = -1e30


def shifted(value, steps):
    count = lax.axis_size("seq")
    first, last = (max(0, -steps), min(count, count - steps))
    return lax.ppermute(value, "seq", [(source, source + steps) for source in range(first, last)])


def swapped(value, axis, flip):
    return lax.ppermute(value, axis, [(i, i ^ flip) for i in range(lax.axis_size(axis))])


def ordered(bit, own, other, axis=0):
    return jnp.where(
        bit == 0,
        jnp.concatenate([own, other], axis=axis),
        jnp.concatenate([other, own], axis=axis),
    )


def body(hidden_in, spike_level, value_weight, queries, key_states, spike_mask, out_grad):
    tok_rows = hidden_in.shape[1]
    chip_rows = 2 * tok_rows
    span = WINDOW + chip_rows
    n_dp, n_seq = lax.axis_size("dp"), lax.axis_size("seq")
    score_scale = 1.0 / math.sqrt(HD)
    place = lax.axis_index("seq")
    core, chip = place % 2, place // 2
    row = lax.axis_index("dp")
    reach = []
    left = WINDOW
    while left > 0:
        reach.append((min(left, chip_rows), len(reach) + 1))
        left -= chip_rows

    def head_half(value):
        half = value.shape[1] // 2
        mine = lax.dynamic_slice_in_dim(value, core * half, half, 1)
        theirs = lax.dynamic_slice_in_dim(value, (1 - core) * half, half, 1)
        return ordered(core, mine, swapped(theirs, "seq", 1))

    def with_past(value):
        pieces = [shifted(value[chip_rows - rows :], 2 * offset) for rows, offset in reach]
        return jnp.concatenate(pieces[::-1] + [value], axis=0)

    def with_future(terms):
        total = terms[WINDOW:]
        begin = WINDOW
        for rows, offset in reach:
            begin -= rows
            got = shifted(terms[begin : begin + rows].astype(jnp.bfloat16), -2 * offset)
            total = total + jnp.pad(got.astype(jnp.float32), ((chip_rows - rows, 0), (0, 0)))
        return total

    key_span = with_past(head_half(key_states[0]))
    weight_half = lax.dynamic_slice_in_dim(value_weight, core * HD, HD, 1)
    if n_dp == 2:
        weight = ordered(row, weight_half, swapped(weight_half, "dp", 1))
    else:
        weight = lax.all_gather(weight_half, "dp", axis=0, tiled=True)
    gated = (
        out_grad[0].reshape(tok_rows, QH, HD) * spike_mask[0][:, :, None].astype(jnp.bfloat16)
    ).reshape(tok_rows, QH * HD)
    gated = head_half(gated).reshape(chip_rows, GROUP, HD)
    query = head_half(queries[0]).reshape(chip_rows, GROUP, HD)
    own_spiked = (
        hidden_in[0].astype(jnp.float32) * (spike_level[0].astype(jnp.float32) / LEVELS)[:, None]
    ).astype(jnp.bfloat16)
    spiked = ordered(core, own_spiked, swapped(own_spiked, "seq", 1))

    query_pos = jnp.arange(chip_rows, dtype=jnp.int32)
    key_pos = jnp.arange(span, dtype=jnp.int32) - WINDOW
    allowed = (
        (key_pos[:, None] <= query_pos[None, :])
        & (key_pos[:, None] > query_pos[None, :] - WINDOW)
        & (key_pos[:, None] >= -chip * chip_rows)
    )
    scores = (
        jnp.einsum("jd,thd->hjt", key_span, query, preferred_element_type=jnp.float32)
        * score_scale
    )
    scores = jnp.where(allowed[None], scores, masked_score)
    expo = jnp.exp(scores - jnp.max(scores, axis=1, keepdims=True))
    probs = expo / jnp.sum(expo, axis=1, keepdims=True)
    rounded_probs = probs.astype(jnp.bfloat16)
    value_terms = jnp.einsum(
        "hjt,thd->jd", rounded_probs, gated, preferred_element_type=jnp.float32
    )
    value_grad = with_future(value_terms).astype(jnp.bfloat16)

    part = lax.dot_general(
        spiked, value_grad, (((0,), (0,)), ((), ())), preferred_element_type=jnp.float32
    )
    steps = [("dp", 1 << b, (row >> b) & 1) for b in range(n_dp.bit_length() - 2, -1, -1)]
    chip_steps = [
        ("seq", 2 << b, (chip >> b) & 1) for b in range((n_seq // 2).bit_length() - 1)
    ]
    for axis, flip, bit in steps + chip_steps:
        half = part.shape[0] // 2
        send = lax.dynamic_slice_in_dim(part, (1 - bit) * half, half, 0).astype(jnp.bfloat16)
        keep = lax.dynamic_slice_in_dim(part, bit * half, half, 0)
        part = keep + swapped(send, axis, flip).astype(jnp.float32)
    owned = part.astype(jnp.bfloat16)
    for axis, flip, bit in chip_steps[::-1]:
        owned = ordered(bit, owned, swapped(owned, axis, flip))
    weight_grad = ordered(core, owned, swapped(owned, "seq", 1), axis=1)

    values = jnp.dot(spiked, weight, preferred_element_type=jnp.float32).astype(jnp.bfloat16)
    value_span = with_past(values)
    prob_grad = jnp.einsum("jd,thd->hjt", value_span, gated, preferred_element_type=jnp.float32)
    delta = jnp.sum(rounded_probs.astype(jnp.float32) * prob_grad, axis=1, keepdims=True)
    score_grad = (probs * (prob_grad - delta)).astype(jnp.bfloat16)
    query_part = (
        jnp.einsum("hjt,jd->thd", score_grad, key_span, preferred_element_type=jnp.float32)
        * score_scale
    ).astype(jnp.bfloat16)
    key_terms = (
        jnp.einsum("hjt,thd->jd", score_grad, query, preferred_element_type=jnp.float32)
        * score_scale
    )
    key_grad = with_future(key_terms).astype(jnp.bfloat16)

    def token_half(value):
        mine = lax.dynamic_slice_in_dim(value, core * tok_rows, tok_rows, 0)
        theirs = lax.dynamic_slice_in_dim(value, (1 - core) * tok_rows, tok_rows, 0)
        return ordered(core, mine, swapped(theirs, "seq", 1), axis=1)

    query_grad = token_half(query_part.reshape(chip_rows, GROUP * HD))
    return (query_grad[None], token_half(key_grad)[None], weight_grad)


def solution(mesh):
    placed = (
        P("dp", "seq", None),
        P("dp", "seq"),
        P("dp", None),
        P("dp", "seq", None),
        P("dp", "seq", None),
        P("dp", "seq", None),
        P("dp", "seq", None),
    )
    return jax.shard_map(
        body,
        mesh=mesh,
        in_specs=placed,
        out_specs=(P("dp", "seq", None), P("dp", "seq", None), P("dp", None)),
        check_vma=False,
    )
```

```python
import functools
import math

import jax
import jax.numpy as jnp
from jax import lax
from jax.experimental import pallas as pl
from jax.experimental.pallas import tpu as pltpu
from jax.sharding import PartitionSpec as P

QH = 14
KVH = 2
HD = 128
WINDOW = 512
LEVELS = 4
GROUP = 7
BLOCK = 128
SPAN = WINDOW + BLOCK

masked_score = -1e30
score_scale = 1.0 / math.sqrt(HD)
exp2_scale = score_scale * math.log2(math.e)

bf16 = jnp.bfloat16
f32 = jnp.float32
ANY = pl.BlockSpec(memory_space=pltpu.HBM)
VMEM = pl.BlockSpec(memory_space=pltpu.VMEM)


def limit(mib):
    return pltpu.CompilerParams(vmem_limit_bytes=mib * 1024 * 1024)


def shifted(value, steps, only=None):
    count = lax.axis_size("seq")
    first, last = (max(0, -steps), min(count, count - steps))
    pairs = [(source, source + steps) for source in range(first, last)]
    if only is not None:
        pairs = [pair for pair in pairs if pair[0] % 2 == only]
    return lax.ppermute(value, "seq", pairs)


def swapped(value, axis, flip):
    return lax.ppermute(value, axis, [(i, i ^ flip) for i in range(lax.axis_size(axis))])


def crossed(value, flips):
    count = lax.axis_size("dp") * lax.axis_size("seq")
    return lax.ppermute(value, ("dp", "seq"), [(i, i ^ flips[i % 2]) for i in range(count)])


def ordered(bit, own, other, axis=0):
    return jnp.where(
        bit == 0,
        jnp.concatenate([own, other], axis=axis),
        jnp.concatenate([other, own], axis=axis),
    )


def run_copies(pairs, sems):
    copies = [pltpu.make_async_copy(src, dst, sems.at[n]) for n, (src, dst) in enumerate(pairs)]
    for copy in copies:
        copy.start()
    return copies


def own_first(core, tok, own, oth, dst, begin=0):
    return [
        (own, dst.at[pl.ds(begin + core * tok, tok)]),
        (oth, dst.at[pl.ds(begin + (1 - core) * tok, tok)]),
    ]


def head_pairs(core, tok, raw, q_buf, g_buf, k_buf):
    q_own, q_oth, g_own, g_oth, k_own, k_oth, p_own, p_oth = raw
    wide = pl.ds(pl.multiple_of(core * GROUP * HD, HD), GROUP * HD)
    slim = pl.ds(pl.multiple_of(core * HD, HD), HD)
    rest = WINDOW - 2 * tok
    pairs = own_first(core, tok, q_own.at[:, wide], q_oth.at[:, wide], q_buf)
    pairs += own_first(core, tok, g_own.at[:, wide], g_oth.at[:, wide], g_buf)
    pairs += own_first(core, tok, k_own.at[:, slim], k_oth.at[:, slim], k_buf, WINDOW)
    pairs += own_first(core, tok, p_own.at[:, slim], p_oth.at[:, slim], k_buf, rest)
    return pairs


def tail_copy(core, tok, far_own, far_oth, k_buf, sem):
    slim = pl.ds(pl.multiple_of(core * HD, HD), HD)
    rest = WINDOW - 2 * tok
    rows = pl.ds(tok - rest, rest)

    @pl.when(core == 1)
    def _():
        pltpu.make_async_copy(far_own.at[rows, slim], k_buf.at[pl.ds(0, rest)], sem).start()

    @pl.when(core == 0)
    def _():
        pltpu.make_async_copy(far_oth.at[rows, slim], k_buf.at[pl.ds(0, rest)], sem).start()

    return pltpu.make_async_copy(far_own.at[rows, slim], k_buf.at[pl.ds(0, rest)], sem)


def head_masks(core, own, oth):
    spikes = jnp.where(
        core == 0,
        jnp.concatenate([own, oth], axis=1),
        jnp.concatenate([oth, own], axis=1),
    ).astype(f32)
    return jnp.where(core == 0, spikes[:GROUP], spikes[GROUP:])


def biases(chip, tok, block):
    later = lax.broadcasted_iota(jnp.int32, (BLOCK, BLOCK), 0)
    query = lax.broadcasted_iota(jnp.int32, (BLOCK, BLOCK), 1)
    first_key = WINDOW - chip * 2 * tok
    tiles = SPAN // BLOCK
    result = []
    for tile in range(tiles):
        begin = (block + tile) * BLOCK
        bias = None
        if begin < WINDOW:
            bias = jnp.where(begin >= first_key, 0.0, masked_score).astype(f32)
        if tile == 0:
            bias = jnp.where(later > query, bias if bias is not None else 0.0, masked_score)
        elif tile == tiles - 1:
            bias = jnp.where(later <= query, 0.0, masked_score)
        result.append(bias)
    return result


def dot_nt(a, b):
    return lax.dot_general(a, b, (((1,), (1,)), ((), ())), preferred_element_type=f32)


def dot_tn(a, b):
    return lax.dot_general(a, b, (((0,), (0,)), ((), ())), preferred_element_type=f32)


def masked(scores, bias):
    tiles = [scores[n * BLOCK : (n + 1) * BLOCK] for n in range(len(bias))]
    return jnp.concatenate(
        [tile if add is None else tile + add for tile, add in zip(tiles, bias)], axis=0
    )


def stacked(buf, block):
    rows = slice(block * BLOCK, (block + 1) * BLOCK)
    return jnp.concatenate(
        [buf[rows, head * HD : (head + 1) * HD] for head in range(GROUP)], axis=0
    )


def value_kernel(tok, *refs):
    raw, far_own, far_oth, m_own, m_oth = refs[:8], *refs[8:12]
    own_out, near_out, far_out, top_out, norm_out = refs[12:17]
    q_buf, g_buf, k_buf, p_buf, acc, sems = refs[17:]
    place = lax.axis_index("seq")
    core, chip = lax.rem(place, 2), lax.div(place, 2)
    copies = run_copies(head_pairs(core, tok, raw, q_buf, g_buf, k_buf), sems)
    copies.append(tail_copy(core, tok, far_own, far_oth, k_buf, sems.at[8]))
    spikes = head_masks(core, m_own[...], m_oth[...])
    acc[...] = jnp.zeros_like(acc)
    for copy in copies:
        copy.wait()
    for block in range(2 * tok // BLOCK):
        bias = biases(chip, tok, block)
        begin = block * BLOCK
        rows = slice(begin, begin + BLOCK)
        keys = k_buf[begin : begin + SPAN, :]
        for head in range(GROUP):
            cols = slice(head * HD, (head + 1) * HD)
            scores = masked(dot_nt(keys, q_buf[rows, cols]), bias)
            top = jnp.max(scores, axis=0, keepdims=True)
            expo = jnp.exp2((scores - top) * exp2_scale)
            norm = spikes[head : head + 1, rows] / jnp.sum(expo, axis=0, keepdims=True)
            p_buf[:, cols] = (expo * norm).astype(bf16)
            at = block * GROUP + head
            top_out[at : at + 1, :] = top
            norm_out[at : at + 1, :] = norm
        acc[begin : begin + SPAN, :] += jnp.dot(
            p_buf[...], stacked(g_buf, block), preferred_element_type=f32
        )
    rest = WINDOW - 2 * tok
    far_out[...] = acc[:rest, :].astype(bf16)
    near_out[...] = acc[rest:WINDOW, :].astype(bf16)
    own_out[...] = acc[WINDOW:, :]


def key_kernel(tok, *refs):
    raw, far_own, far_oth = refs[:8], refs[8], refs[9]
    top_in, norm_in, v_own, v_near, v_far = refs[10:15]
    own_out, near_out, far_out, mine_out, send_out = refs[15:20]
    q_buf, g_buf, k_buf, v_buf, d_buf, acc, r_buf, sems, out_sems = refs[20:]
    place = lax.axis_index("seq")
    core, chip = lax.rem(place, 2), lax.div(place, 2)
    rest = WINDOW - 2 * tok
    pairs = head_pairs(core, tok, raw, q_buf, g_buf, k_buf)
    pairs += [
        (v_far, v_buf.at[pl.ds(0, rest)]),
        (v_near, v_buf.at[pl.ds(rest, 2 * tok)]),
        (v_own, v_buf.at[pl.ds(WINDOW, 2 * tok)]),
    ]
    copies = run_copies(pairs, sems)
    copies.append(tail_copy(core, tok, far_own, far_oth, k_buf, sems.at[len(pairs)]))
    acc[...] = jnp.zeros_like(acc)
    for copy in copies:
        copy.wait()
    for block in range(2 * tok // BLOCK):
        bias = biases(chip, tok, block)
        begin = block * BLOCK
        rows = slice(begin, begin + BLOCK)
        keys = k_buf[begin : begin + SPAN, :]
        values = v_buf[begin : begin + SPAN, :]
        for head in range(GROUP):
            cols = slice(head * HD, (head + 1) * HD)
            at = block * GROUP + head
            scores = masked(dot_nt(keys, q_buf[rows, cols]), bias)
            probs = jnp.exp2((scores - top_in[at : at + 1, :]) * exp2_scale)
            probs = probs * norm_in[at : at + 1, :]
            prob_grad = dot_nt(values, g_buf[rows, cols])
            delta = jnp.sum(probs.astype(bf16).astype(f32) * prob_grad, axis=0, keepdims=True)
            d_buf[:, cols] = (probs * (prob_grad - delta)).astype(bf16)
        acc[begin : begin + SPAN, :] += jnp.dot(
            d_buf[...], stacked(q_buf, block), preferred_element_type=f32
        )
        query_part = dot_tn(d_buf[...], keys) * score_scale
        for head in range(GROUP):
            cols = slice(head * HD, (head + 1) * HD)
            r_buf[rows, cols] = query_part[head * BLOCK : (head + 1) * BLOCK].astype(bf16)
    mine = pltpu.make_async_copy(r_buf.at[pl.ds(core * tok, tok)], mine_out, out_sems.at[0])
    send = pltpu.make_async_copy(r_buf.at[pl.ds((1 - core) * tok, tok)], send_out, out_sems.at[1])
    mine.start()
    send.start()
    far_out[...] = (acc[:rest, :] * score_scale).astype(bf16)
    near_out[...] = (acc[rest:WINDOW, :] * score_scale).astype(bf16)
    own_out[...] = acc[WINDOW:, :] * score_scale
    mine.wait()
    send.wait()


def head_scratch(tok):
    return [
        pltpu.VMEM((2 * tok, GROUP * HD), bf16),
        pltpu.VMEM((2 * tok, GROUP * HD), bf16),
        pltpu.VMEM((WINDOW + 2 * tok, HD), bf16),
    ]


def term_shapes(tok):
    return [
        jax.ShapeDtypeStruct((2 * tok, HD), f32),
        jax.ShapeDtypeStruct((2 * tok, HD), bf16),
        jax.ShapeDtypeStruct((WINDOW - 2 * tok, HD), bf16),
    ]


def value_terms(tok, raw, spikes):
    stats = jax.ShapeDtypeStruct((2 * tok // BLOCK * GROUP, BLOCK), f32)
    return pl.pallas_call(
        functools.partial(value_kernel, tok),
        out_shape=term_shapes(tok) + [stats, stats],
        in_specs=[ANY] * 10 + [VMEM] * 2,
        out_specs=[VMEM] * 5,
        scratch_shapes=head_scratch(tok)
        + [
            pltpu.VMEM((SPAN, GROUP * HD), bf16),
            pltpu.VMEM((WINDOW + 2 * tok, HD), f32),
            pltpu.SemaphoreType.DMA((9,)),
        ],
        compiler_params=limit(12),
        name="value_terms",
    )(*raw, *spikes)


def key_terms(tok, raw, top, norm, values):
    half = jax.ShapeDtypeStruct((tok, GROUP * HD), bf16)
    return pl.pallas_call(
        functools.partial(key_kernel, tok),
        out_shape=term_shapes(tok) + [half, half],
        in_specs=[ANY] * 10 + [VMEM] * 2 + [ANY] * 3,
        out_specs=[VMEM] * 3 + [ANY] * 2,
        scratch_shapes=head_scratch(tok)
        + [
            pltpu.VMEM((WINDOW + 2 * tok, HD), bf16),
            pltpu.VMEM((SPAN, GROUP * HD), bf16),
            pltpu.VMEM((WINDOW + 2 * tok, HD), f32),
            pltpu.VMEM((2 * tok, GROUP * HD), bf16),
            pltpu.SemaphoreType.DMA((12,)),
            pltpu.SemaphoreType.DMA((2,)),
        ],
        compiler_params=limit(14),
        name="key_terms",
    )(*raw, top, norm, *values)


def column(row):
    size = row.shape[1]
    diagonal = lax.broadcasted_iota(jnp.int32, (size, size), 0) == lax.broadcasted_iota(
        jnp.int32, (size, size), 1
    )
    return jnp.sum(jnp.where(diagonal, row, 0.0), axis=1, keepdims=True)


def project_kernel(tok, split, h_own, h_oth, l_own, l_oth, w_own, w_oth, out, tail, spiked, w_buf, sems):
    core = lax.rem(lax.axis_index("seq"), 2)
    if split:
        row = lax.axis_index("dp")
        depth = w_own.shape[0]
        pairs = [
            (w_own, w_buf.at[pl.ds(pl.multiple_of(row * depth, depth), depth)]),
            (w_oth, w_buf.at[pl.ds(pl.multiple_of((1 - row) * depth, depth), depth)]),
        ]
    else:
        pairs = [(w_own, w_buf)]
    copies = run_copies(pairs, sems)
    for source, level, place in ((h_own, l_own, core), (h_oth, l_oth, 1 - core)):
        factor = column(level[...].astype(f32) / LEVELS)
        rows = pl.ds(pl.multiple_of(place * tok, 64), tok)
        spiked[rows, :] = (source[...].astype(f32) * factor).astype(bf16)
    for copy in copies:
        copy.wait()
    values = jnp.dot(spiked[...], w_buf[...], preferred_element_type=f32).astype(bf16)
    out[...] = values
    tail[...] = values[4 * tok - WINDOW :, :]


def project(tok, hidden, levels, weight):
    depth = hidden[0].shape[1]
    split = len(weight) == 2
    return pl.pallas_call(
        functools.partial(project_kernel, tok, split),
        out_shape=[
            jax.ShapeDtypeStruct((2 * tok, HD), bf16),
            jax.ShapeDtypeStruct((WINDOW - 2 * tok, HD), bf16),
            jax.ShapeDtypeStruct((2 * tok, depth), bf16),
        ],
        in_specs=[VMEM] * 4 + [ANY] * 2,
        out_specs=[VMEM] * 3,
        scratch_shapes=[pltpu.VMEM((depth, HD), bf16), pltpu.SemaphoreType.DMA((2,))],
        compiler_params=limit(14),
        name="project",
    )(*hidden, *levels, weight[0], weight[-1])


def value_sum(tok, own, near, far):
    late = own[4 * tok - WINDOW :] + far.astype(f32)
    early = own[: 4 * tok - WINDOW]
    return jnp.concatenate([early, late], axis=0) + near.astype(f32)


def weight_kernel(tok, spiked, own, near, far, keep, send, w_buf):
    core = lax.rem(lax.axis_index("seq"), 2)
    rows = spiked.shape[1] // 16
    value_grad = value_sum(tok, own[...], near[...], far[...]).astype(bf16)
    mine = block_code(core)
    for part in range(4):
        term = dot_tn(spiked[:, part * 4 * rows : (part + 1) * 4 * rows], value_grad)
        for piece in range(4):
            index = part * 4 + piece
            other = (index & 3) | ((index & 4) << 1) | ((index & 8) >> 1)
            at = jnp.where(core == 0, index, other) ^ mine
            w_buf[pl.ds(pl.multiple_of(at * rows, 16), rows), :] = term[
                piece * rows : (piece + 1) * rows
            ]
    keep[...] = w_buf[: 8 * rows, :]
    send[...] = w_buf[8 * rows :, :].astype(bf16)


def chip_bits():
    chip = lax.div(lax.axis_index("seq"), 2)
    return chip & 1, (chip >> 1) & 1, (chip >> 2) & 1


def block_code(core):
    y, near, far = chip_bits()
    row = lax.axis_index("dp")
    return jnp.where(
        core == 0,
        row * 8 + y * 4 + near * 2 + far,
        near * 8 + row * 4 + y * 2 + far,
    )


def chip_code(core):
    y, near, far = chip_bits()
    return jnp.where(core == 0, y * 4 + near * 2 + far, near * 4 + y * 2 + far)


def weight_terms(tok, spiked, terms):
    depth = spiked.shape[1]
    return pl.pallas_call(
        functools.partial(weight_kernel, tok),
        out_shape=[
            jax.ShapeDtypeStruct((depth // 2, HD), f32),
            jax.ShapeDtypeStruct((depth // 2, HD), bf16),
        ],
        in_specs=[VMEM] * 4,
        out_specs=[VMEM] * 2,
        scratch_shapes=[pltpu.VMEM((depth, HD), f32)],
        compiler_params=limit(14),
        name="weight_terms",
    )(spiked, *terms)


def halve_kernel(held, got, *outs):
    total = held[...] + got[...].astype(f32)
    half = total.shape[0] // 2
    if len(outs) == 2:
        outs[0][...] = total[:half]
        outs[1][...] = total[half:].astype(bf16)
    else:
        outs[0][...] = total.astype(bf16)


def halve(held, got, last=False):
    rows = held.shape[0]
    if last:
        shapes = [jax.ShapeDtypeStruct((rows, HD), bf16)]
    else:
        shapes = [
            jax.ShapeDtypeStruct((rows // 2, HD), f32),
            jax.ShapeDtypeStruct((rows // 2, HD), bf16),
        ]
    return pl.pallas_call(
        halve_kernel,
        out_shape=shapes,
        in_specs=[VMEM] * 2,
        out_specs=[VMEM] * len(shapes),
        compiler_params=limit(6),
        name="halve",
    )(held, got)


def join_kernel(first, second, out):
    rows = first.shape[0]
    out[:rows, :] = first[...]
    out[rows:, :] = second[...]


def join(first, second):
    return pl.pallas_call(
        join_kernel,
        out_shape=jax.ShapeDtypeStruct((2 * first.shape[0], HD), bf16),
        in_specs=[VMEM] * 2,
        out_specs=VMEM,
        compiler_params=limit(4),
        name="join",
    )(first, second)


def place_weight_kernel(own_low, own_high, oth_low, oth_high, out, sems):
    core = lax.rem(lax.axis_index("seq"), 2)
    rows = own_low.shape[0] // 4
    pairs = []
    for halves, side in (((own_low, own_high), core), ((oth_low, oth_high), 1 - core)):
        code = chip_code(side)
        cols = pl.ds(pl.multiple_of(side * HD, HD), HD)
        for index in range(8):
            source = halves[index // 4].at[pl.ds(index % 4 * rows, rows)]
            at = pl.ds(pl.multiple_of((index ^ code) * rows, 16), rows)
            pairs.append((source, out.at[at, cols]))
    for copy in run_copies(pairs, sems):
        copy.wait()


def place_weight(*pieces):
    return pl.pallas_call(
        place_weight_kernel,
        out_shape=jax.ShapeDtypeStruct((2 * pieces[0].shape[0], KVH * HD), bf16),
        in_specs=[ANY] * 4,
        out_specs=ANY,
        scratch_shapes=[pltpu.SemaphoreType.DMA((16,))],
        compiler_params=limit(2),
        name="place_weight",
    )(*pieces)


def place_tokens_kernel(q_own, q_oth, k_own, k_oth, q_out, k_out, sems):
    core = lax.rem(lax.axis_index("seq"), 2)
    pairs = []
    for own, oth, out in ((q_own, q_oth, q_out), (k_own, k_oth, k_out)):
        width = own.shape[1]
        for source, side in ((own, core), (oth, 1 - core)):
            cols = pl.ds(pl.multiple_of(side * width, HD), width)
            pairs.append((source, out.at[:, cols]))
    for copy in run_copies(pairs, sems):
        copy.wait()


def place_tokens(q_own, q_oth, k_own, k_oth):
    return pl.pallas_call(
        place_tokens_kernel,
        out_shape=[
            jax.ShapeDtypeStruct((own.shape[0], 2 * own.shape[1]), bf16) for own in (q_own, k_own)
        ],
        in_specs=[ANY] * 4,
        out_specs=[ANY] * 2,
        scratch_shapes=[pltpu.SemaphoreType.DMA((4,))],
        compiler_params=limit(2),
        name="place_tokens",
    )(q_own, q_oth, k_own, k_oth)


def reduce_any(spiked, value_grad, core, place, row):
    n_dp, n_seq = lax.axis_size("dp"), lax.axis_size("seq")
    chip = place // 2
    part = lax.dot_general(
        spiked, value_grad, (((0,), (0,)), ((), ())), preferred_element_type=f32
    )
    steps = [("dp", 1 << b, (row >> b) & 1) for b in range(n_dp.bit_length() - 2, -1, -1)]
    chip_steps = [
        ("seq", 2 << b, (chip >> b) & 1) for b in range((n_seq // 2).bit_length() - 1)
    ]
    for axis, flip, bit in steps + chip_steps:
        half = part.shape[0] // 2
        send = lax.dynamic_slice_in_dim(part, (1 - bit) * half, half, 0).astype(bf16)
        keep = lax.dynamic_slice_in_dim(part, bit * half, half, 0)
        part = keep + swapped(send, axis, flip).astype(f32)
    owned = part.astype(bf16)
    for axis, flip, bit in chip_steps[::-1]:
        owned = ordered(bit, owned, swapped(owned, axis, flip))
    return ordered(core, owned, swapped(owned, "seq", 1), axis=1)


def after(value, *others):
    return lax.optimization_barrier((value, *others))[0]


def body(hidden_in, spike_level, value_weight, queries, key_states, spike_mask, out_grad):
    tok = hidden_in.shape[1]
    n_dp, n_seq = lax.axis_size("dp"), lax.axis_size("seq")
    place, row = lax.axis_index("seq"), lax.axis_index("dp")
    core = place % 2
    assert 0 < WINDOW - 2 * tok <= tok and 2 * tok % BLOCK == 0

    def both(value):
        return value, swapped(value, "seq", 1)

    own_keys = key_states[0]
    near_keys, far_keys = lax.optimization_barrier(
        (shifted(own_keys, 2), shifted(own_keys, 4, only=1))
    )
    weight_half = lax.dynamic_slice_in_dim(value_weight, core * HD, HD, 1)
    raw = []
    for mine in (queries[0], out_grad[0], own_keys, near_keys, far_keys):
        raw += both(mine)
    if n_dp == 2:
        weight = (weight_half, swapped(weight_half, "dp", 1))
    else:
        weight = (lax.all_gather(weight_half, "dp", axis=0, tiled=True),)

    own, near, far, top, norm = value_terms(tok, raw, both(jnp.transpose(spike_mask[0])))
    near, far = shifted(near, -2), shifted(far, -4)
    values, tail, spiked = project(tok, both(hidden_in[0]), both(spike_level), weight)

    fast = n_dp == 2 and n_seq == 16 and hidden_in.shape[2] % 256 == 0
    if fast:
        keep, send = weight_terms(tok, spiked, (own, near, far))
        values, tail = lax.optimization_barrier((values, tail, send))[:2]
        got = crossed(send, (n_seq, 4))
    window = (values, shifted(values, 2), shifted(tail, 4))
    if fast:
        keep, send = halve(keep, after(got, *window))
        window = lax.optimization_barrier((*window, send))[:3]
        got = crossed(send, (2, n_seq))
    own_k, near_k, far_k, query_mine, query_send = key_terms(tok, raw, top, norm, window)
    if fast:
        keep, send = halve(keep, after(got, own_k))
        near_k, far_k = lax.optimization_barrier((near_k, far_k, send))[:2]
        got = crossed(send, (4, 2))
    near_k, far_k = shifted(near_k, -2), shifted(far_k, -4)
    query_got = swapped(query_send, "seq", 1)
    if fast:
        keep, send = halve(keep, after(got, near_k, far_k))
        near_k, far_k = lax.optimization_barrier((near_k, far_k, send))[:2]
        got = crossed(send, (8, 8))
    key_grad = value_sum(tok, own_k, near_k, far_k).astype(bf16)
    key_mine = lax.dynamic_slice_in_dim(key_grad, core * tok, tok, 0)
    key_send = lax.dynamic_slice_in_dim(key_grad, (1 - core) * tok, tok, 0)
    query_grad, key_grad = place_tokens(
        query_mine, query_got, key_mine, swapped(key_send, "seq", 1)
    )
    if fast:
        (owned,) = halve(keep, after(got, query_grad), last=True)
        owned = join(owned, crossed(owned, (8, 8)))
        owned = join(owned, crossed(owned, (4, 2)))
        rest = crossed(owned, (2, 4))
        weight_grad = place_weight(
            owned, rest, swapped(owned, "seq", 1), swapped(rest, "seq", 1)
        )
    else:
        value_grad = value_sum(tok, own, near, far).astype(bf16)
        weight_grad = reduce_any(spiked, value_grad, core, place, row)
    return (query_grad[None], key_grad[None], weight_grad)


def solution(mesh):
    placed = (
        P("dp", "seq", None),
        P("dp", "seq"),
        P("dp", None),
        P("dp", "seq", None),
        P("dp", "seq", None),
        P("dp", "seq", None),
        P("dp", "seq", None),
    )
    return jax.shard_map(
        body,
        mesh=mesh,
        in_specs=placed,
        out_specs=(P("dp", "seq", None), P("dp", "seq", None), P("dp", None)),
        check_vma=False,
    )
```

```python
import functools
import math

import jax
import jax.numpy as jnp
from jax import lax
from jax.experimental import pallas as pl
from jax.experimental.pallas import tpu as pltpu
from jax.sharding import PartitionSpec as P

QH = 14
KVH = 2
HD = 128
WINDOW = 512
LEVELS = 4
GROUP = 7
BLOCK = 128
SPAN = WINDOW + BLOCK

masked_score = -1e30
score_scale = 1.0 / math.sqrt(HD)
exp2_scale = score_scale * math.log2(math.e)

bf16 = jnp.bfloat16
f32 = jnp.float32
ANY = pl.BlockSpec(memory_space=pltpu.HBM)
VMEM = pl.BlockSpec(memory_space=pltpu.VMEM)


def limit(mib):
    return pltpu.CompilerParams(vmem_limit_bytes=mib * 1024 * 1024)


def shifted(value, steps):
    count = lax.axis_size("seq")
    return lax.ppermute(value, "seq", [(i, (i + steps) % count) for i in range(count)])


def swapped(value, axis, flip):
    return lax.ppermute(value, axis, [(i, i ^ flip) for i in range(lax.axis_size(axis))])


def crossed(value, flips):
    count = lax.axis_size("dp") * lax.axis_size("seq")
    return lax.ppermute(value, ("dp", "seq"), [(i, i ^ flips[i % 2]) for i in range(count)])


def ordered(bit, own, other, axis=0):
    return jnp.where(
        bit == 0,
        jnp.concatenate([own, other], axis=axis),
        jnp.concatenate([other, own], axis=axis),
    )


def run_copies(pairs, sems):
    copies = [pltpu.make_async_copy(src, dst, sems.at[n]) for n, (src, dst) in enumerate(pairs)]
    for copy in copies:
        copy.start()
    return copies


def split_kernel(
    tok, q_ref, g_ref, m_ref, l_ref, q_own, q_send, g_own, g_send, marks, m_buf, l_buf, sems
):
    core = lax.rem(lax.axis_index("seq"), 2)
    wide = GROUP * HD
    pairs = [(m_ref, m_buf), (l_ref, l_buf)]
    for source, own, send in ((q_ref, q_own, q_send), (g_ref, g_own, g_send)):
        for target, side in ((own, core), (send, 1 - core)):
            pairs.append((source.at[:, pl.ds(pl.multiple_of(side * wide, HD), wide)], target))
    copies = run_copies(pairs, sems)
    for copy in copies:
        copy.wait()
    for head in range(QH):
        marks[head : head + 1, :] = m_buf[head]
    marks[QH : QH + 1, :] = l_buf[...]


def in_hbm(value):
    return pltpu.with_memory_space_constraint(value, pltpu.HBM)


def split(tok, query, grad, spikes, level):
    half = jax.ShapeDtypeStruct((tok, GROUP * HD), bf16)
    return pl.pallas_call(
        functools.partial(split_kernel, tok),
        out_shape=[half] * 4 + [jax.ShapeDtypeStruct((QH + 1, tok), jnp.int32)],
        in_specs=[ANY] * 4,
        out_specs=[VMEM] * 5,
        scratch_shapes=[
            pltpu.VMEM((QH, 1, tok), jnp.int32),
            pltpu.VMEM((1, tok), jnp.int32),
            pltpu.SemaphoreType.DMA((6,)),
        ],
        compiler_params=limit(4),
        name="split",
    )(in_hbm(query), in_hbm(grad), in_hbm(spikes), in_hbm(level))


def pack_kernel(tok, own, near, far, mine, send, sems):
    core = lax.rem(lax.axis_index("seq"), 2)
    rest = WINDOW - 2 * tok
    sides = ((mine, core), (send, 1 - core))
    pairs = []
    for target, side in sides:
        cols = pl.ds(pl.multiple_of(side * HD, HD), HD)
        pairs.append((own.at[:, cols], target.at[pl.ds(rest + tok, tok)]))
    copies = run_copies(pairs, sems)
    for target, side in sides:
        cols = pl.ds(pl.multiple_of(side * HD, HD), HD)
        target[:rest, :] = far[tok - rest :, cols]
        target[rest : rest + tok, :] = near[:, cols]
    for copy in copies:
        copy.wait()


def pack(tok, own, near, far):
    half = jax.ShapeDtypeStruct((WINDOW, HD), bf16)
    return pl.pallas_call(
        functools.partial(pack_kernel, tok),
        out_shape=[half] * 2,
        in_specs=[ANY] + [VMEM] * 2,
        out_specs=[VMEM] * 2,
        scratch_shapes=[pltpu.SemaphoreType.DMA((2,))],
        compiler_params=limit(4),
        name="pack",
    )(in_hbm(own), near, far)


def lay_out(core, tok, raw, q_buf, g_buf, k_buf):
    q_own, q_oth, g_own, g_oth, k_own, k_oth = raw
    rest = WINDOW - 2 * tok
    for own, oth, buf, first, begin in (
        (k_own, k_oth, k_buf, rest, rest),
        (k_own, k_oth, k_buf, rest + tok, WINDOW),
        (q_own, q_oth, q_buf, 0, 0),
        (g_own, g_oth, g_buf, 0, 0),
    ):
        buf[pl.ds(pl.multiple_of(begin + core * tok, 64), tok), :] = own[first : first + tok, :]
        buf[pl.ds(pl.multiple_of(begin + (1 - core) * tok, 64), tok), :] = oth[
            first : first + tok, :
        ]
    k_buf[:rest, :] = jnp.where(core == 1, k_own[:rest, :], k_oth[:rest, :])


def head_masks(core, own, oth):
    spikes = jnp.where(
        core == 0,
        jnp.concatenate([own, oth], axis=1),
        jnp.concatenate([oth, own], axis=1),
    ).astype(f32)
    return jnp.where(core == 0, spikes[:GROUP], spikes[GROUP:])


def biases(chip, tok, block):
    later = lax.broadcasted_iota(jnp.int32, (BLOCK, BLOCK), 0)
    query = lax.broadcasted_iota(jnp.int32, (BLOCK, BLOCK), 1)
    first_key = WINDOW - chip * 2 * tok
    tiles = SPAN // BLOCK
    result = []
    for tile in range(tiles):
        begin = (block + tile) * BLOCK
        bias = None
        if begin < WINDOW:
            bias = jnp.where(begin >= first_key, 0.0, masked_score).astype(f32)
        if tile == 0:
            bias = jnp.where(later > query, bias if bias is not None else 0.0, masked_score)
        elif tile == tiles - 1:
            bias = jnp.where(later <= query, 0.0, masked_score)
        result.append(bias)
    return result


def dot_nt(a, b):
    return lax.dot_general(a, b, (((1,), (1,)), ((), ())), preferred_element_type=f32)


def dot_tn(a, b):
    return lax.dot_general(a, b, (((0,), (0,)), ((), ())), preferred_element_type=f32)


def masked(scores, bias):
    tiles = [scores[n * BLOCK : (n + 1) * BLOCK] for n in range(len(bias))]
    return jnp.concatenate(
        [tile if add is None else tile + add for tile, add in zip(tiles, bias)], axis=0
    )


def stacked(buf, block):
    rows = slice(block * BLOCK, (block + 1) * BLOCK)
    return jnp.concatenate(
        [buf[rows, head * HD : (head + 1) * HD] for head in range(GROUP)], axis=0
    )


def value_kernel(tok, *refs):
    raw, m_own, m_oth = refs[:6], *refs[6:8]
    own_out, near_out, far_out, top_out, norm_out = refs[8:13]
    q_buf, g_buf, k_buf, p_buf, acc = refs[13:]
    place = lax.axis_index("seq")
    core, chip = lax.rem(place, 2), lax.div(place, 2)
    lay_out(core, tok, raw, q_buf, g_buf, k_buf)
    spikes = head_masks(core, m_own[:QH, :], m_oth[:QH, :])
    acc[...] = jnp.zeros_like(acc)
    for block in range(2 * tok // BLOCK):
        bias = biases(chip, tok, block)
        begin = block * BLOCK
        rows = slice(begin, begin + BLOCK)
        keys = k_buf[begin : begin + SPAN, :]
        for head in range(GROUP):
            cols = slice(head * HD, (head + 1) * HD)
            scores = masked(dot_nt(keys, q_buf[rows, cols]), bias)
            top = jnp.max(scores, axis=0, keepdims=True)
            expo = jnp.exp2((scores - top) * exp2_scale)
            norm = spikes[head : head + 1, rows] / jnp.sum(expo, axis=0, keepdims=True)
            p_buf[:, cols] = (expo * norm).astype(bf16)
            at = block * GROUP + head
            top_out[at : at + 1, :] = top
            norm_out[at : at + 1, :] = norm
        acc[begin : begin + SPAN, :] += jnp.dot(
            p_buf[...], stacked(g_buf, block), preferred_element_type=f32
        )
    rest = WINDOW - 2 * tok
    far_out[...] = acc[:rest, :].astype(bf16)
    near_out[...] = acc[rest:WINDOW, :].astype(bf16)
    own_out[...] = acc[WINDOW:, :]


def key_kernel(tok, *refs):
    raw = refs[:6]
    top_in, norm_in, v_own, v_near, v_far = refs[6:11]
    own_out, near_out, far_out, mine_out, send_out = refs[11:16]
    q_buf, g_buf, k_buf, v_buf, d_buf, acc, r_buf = refs[16:]
    place = lax.axis_index("seq")
    core, chip = lax.rem(place, 2), lax.div(place, 2)
    rest = WINDOW - 2 * tok
    lay_out(core, tok, raw, q_buf, g_buf, k_buf)
    v_buf[:rest, :] = v_far[...]
    v_buf[rest:WINDOW, :] = v_near[...]
    v_buf[WINDOW:, :] = v_own[...]
    acc[...] = jnp.zeros_like(acc)
    for block in range(2 * tok // BLOCK):
        bias = biases(chip, tok, block)
        begin = block * BLOCK
        rows = slice(begin, begin + BLOCK)
        keys = k_buf[begin : begin + SPAN, :]
        values = v_buf[begin : begin + SPAN, :]
        for head in range(GROUP):
            cols = slice(head * HD, (head + 1) * HD)
            at = block * GROUP + head
            scores = masked(dot_nt(keys, q_buf[rows, cols]), bias)
            probs = jnp.exp2((scores - top_in[at : at + 1, :]) * exp2_scale)
            probs = probs * norm_in[at : at + 1, :]
            prob_grad = dot_nt(values, g_buf[rows, cols])
            delta = jnp.sum(probs.astype(bf16).astype(f32) * prob_grad, axis=0, keepdims=True)
            d_buf[:, cols] = (probs * (prob_grad - delta)).astype(bf16)
        acc[begin : begin + SPAN, :] += jnp.dot(
            d_buf[...], stacked(q_buf, block), preferred_element_type=f32
        )
        query_part = dot_tn(d_buf[...], keys) * score_scale
        for head in range(GROUP):
            cols = slice(head * HD, (head + 1) * HD)
            r_buf[rows, cols] = query_part[head * BLOCK : (head + 1) * BLOCK].astype(bf16)
    mine_out[...] = r_buf[pl.ds(pl.multiple_of(core * tok, 64), tok), :]
    send_out[...] = r_buf[pl.ds(pl.multiple_of((1 - core) * tok, 64), tok), :]
    far_out[...] = (acc[:rest, :] * score_scale).astype(bf16)
    near_out[...] = (acc[rest:WINDOW, :] * score_scale).astype(bf16)
    own_out[...] = acc[WINDOW:, :] * score_scale


def head_scratch(tok):
    return [
        pltpu.VMEM((2 * tok, GROUP * HD), bf16),
        pltpu.VMEM((2 * tok, GROUP * HD), bf16),
        pltpu.VMEM((WINDOW + 2 * tok, HD), bf16),
    ]


def term_shapes(tok):
    return [
        jax.ShapeDtypeStruct((2 * tok, HD), f32),
        jax.ShapeDtypeStruct((2 * tok, HD), bf16),
        jax.ShapeDtypeStruct((WINDOW - 2 * tok, HD), bf16),
    ]


def value_terms(tok, raw, spikes):
    stats = jax.ShapeDtypeStruct((2 * tok // BLOCK * GROUP, BLOCK), f32)
    return pl.pallas_call(
        functools.partial(value_kernel, tok),
        out_shape=term_shapes(tok) + [stats, stats],
        in_specs=[VMEM] * 8,
        out_specs=[VMEM] * 5,
        scratch_shapes=head_scratch(tok)
        + [
            pltpu.VMEM((SPAN, GROUP * HD), bf16),
            pltpu.VMEM((WINDOW + 2 * tok, HD), f32),
        ],
        compiler_params=limit(12),
        name="value_terms",
    )(*raw, *spikes)


def key_terms(tok, raw, top, norm, values):
    half = jax.ShapeDtypeStruct((tok, GROUP * HD), bf16)
    return pl.pallas_call(
        functools.partial(key_kernel, tok),
        out_shape=term_shapes(tok) + [half, half],
        in_specs=[VMEM] * 11,
        out_specs=[VMEM] * 5,
        scratch_shapes=head_scratch(tok)
        + [
            pltpu.VMEM((WINDOW + 2 * tok, HD), bf16),
            pltpu.VMEM((SPAN, GROUP * HD), bf16),
            pltpu.VMEM((WINDOW + 2 * tok, HD), f32),
            pltpu.VMEM((2 * tok, GROUP * HD), bf16),
        ],
        compiler_params=limit(14),
        name="key_terms",
    )(*raw, top, norm, *values)


def sum_keys_kernel(tok, own, near, far, mine, send, buf):
    core = lax.rem(lax.axis_index("seq"), 2)
    buf[...] = value_sum(tok, own[...], near[...], far[...])
    mine[...] = buf[pl.ds(pl.multiple_of(core * tok, 64), tok), :].astype(bf16)
    send[...] = buf[pl.ds(pl.multiple_of((1 - core) * tok, 64), tok), :].astype(bf16)


def sum_keys(tok, own, near, far):
    half = jax.ShapeDtypeStruct((tok, HD), bf16)
    return pl.pallas_call(
        functools.partial(sum_keys_kernel, tok),
        out_shape=[half, half],
        in_specs=[VMEM] * 3,
        out_specs=[VMEM] * 2,
        scratch_shapes=[pltpu.VMEM((2 * tok, HD), f32)],
        compiler_params=limit(4),
        name="sum_keys",
    )(own, near, far)


def column(row):
    size = row.shape[1]
    diagonal = lax.broadcasted_iota(jnp.int32, (size, size), 0) == lax.broadcasted_iota(
        jnp.int32, (size, size), 1
    )
    return jnp.sum(jnp.where(diagonal, row, 0.0), axis=1, keepdims=True)


def project_kernel(tok, split, h_own, h_oth, l_own, l_oth, w_own, w_oth, out, tail, spiked, w_buf, sems):
    core = lax.rem(lax.axis_index("seq"), 2)
    if split:
        row = lax.axis_index("dp")
        depth = w_own.shape[0]
        pairs = [
            (w_own, w_buf.at[pl.ds(pl.multiple_of(row * depth, depth), depth)]),
            (w_oth, w_buf.at[pl.ds(pl.multiple_of((1 - row) * depth, depth), depth)]),
        ]
    else:
        pairs = [(w_own, w_buf)]
    copies = run_copies(pairs, sems)
    for source, level, place in ((h_own, l_own, core), (h_oth, l_oth, 1 - core)):
        factor = column(level[QH : QH + 1, :].astype(f32) / LEVELS)
        rows = pl.ds(pl.multiple_of(place * tok, 64), tok)
        spiked[rows, :] = (source[...].astype(f32) * factor).astype(bf16)
    for copy in copies:
        copy.wait()
    values = jnp.dot(spiked[...], w_buf[...], preferred_element_type=f32).astype(bf16)
    out[...] = values
    tail[...] = values[4 * tok - WINDOW :, :]


def project(tok, hidden, levels, weight):
    depth = hidden[0].shape[1]
    split = len(weight) == 2
    return pl.pallas_call(
        functools.partial(project_kernel, tok, split),
        out_shape=[
            jax.ShapeDtypeStruct((2 * tok, HD), bf16),
            jax.ShapeDtypeStruct((WINDOW - 2 * tok, HD), bf16),
            jax.ShapeDtypeStruct((2 * tok, depth), bf16),
        ],
        in_specs=[VMEM] * 4 + [ANY] * 2,
        out_specs=[VMEM] * 3,
        scratch_shapes=[pltpu.VMEM((depth, HD), bf16), pltpu.SemaphoreType.DMA((2,))],
        compiler_params=limit(14),
        name="project",
    )(*hidden, *levels, weight[0], weight[-1])


def value_sum(tok, own, near, far):
    late = own[4 * tok - WINDOW :] + far.astype(f32)
    early = own[: 4 * tok - WINDOW]
    return jnp.concatenate([early, late], axis=0) + near.astype(f32)


def weight_kernel(tok, spiked, own, near, far, keep, send, w_buf):
    core = lax.rem(lax.axis_index("seq"), 2)
    rows = spiked.shape[1] // 16
    value_grad = value_sum(tok, own[...], near[...], far[...]).astype(bf16)
    mine = block_code(core)
    for part in range(4):
        term = dot_tn(spiked[:, part * 4 * rows : (part + 1) * 4 * rows], value_grad)
        for piece in range(4):
            at = (part * 4 + piece) ^ mine
            w_buf[pl.ds(pl.multiple_of(at * rows, 16), rows), :] = term[
                piece * rows : (piece + 1) * rows
            ]
    keep[...] = w_buf[: 8 * rows, :]
    send[...] = w_buf[8 * rows :, :].astype(bf16)


def chip_bits():
    chip = lax.div(lax.axis_index("seq"), 2)
    return chip & 1, (chip >> 1) & 1, (chip >> 2) & 1


def block_code(core):
    return lax.axis_index("dp") * 8 + chip_code(core)


def chip_code(core):
    y, near, far = chip_bits()
    return jnp.where(core == 0, y * 4 + near * 2 + far, near * 4 + y * 2 + far)


def weight_terms(tok, spiked, terms):
    depth = spiked.shape[1]
    return pl.pallas_call(
        functools.partial(weight_kernel, tok),
        out_shape=[
            jax.ShapeDtypeStruct((depth // 2, HD), f32),
            jax.ShapeDtypeStruct((depth // 2, HD), bf16),
        ],
        in_specs=[VMEM] * 4,
        out_specs=[VMEM] * 2,
        scratch_shapes=[pltpu.VMEM((depth, HD), f32)],
        compiler_params=limit(14),
        name="weight_terms",
    )(spiked, *terms)


def halve_kernel(held, got, *outs):
    total = held[...] + got[...].astype(f32)
    half = total.shape[0] // 2
    if len(outs) == 2:
        outs[0][...] = total[:half]
        outs[1][...] = total[half:].astype(bf16)
    else:
        outs[0][...] = total.astype(bf16)


def halve(held, got, last=False):
    rows = held.shape[0]
    if last:
        shapes = [jax.ShapeDtypeStruct((rows, HD), bf16)]
    else:
        shapes = [
            jax.ShapeDtypeStruct((rows // 2, HD), f32),
            jax.ShapeDtypeStruct((rows // 2, HD), bf16),
        ]
    return pl.pallas_call(
        halve_kernel,
        out_shape=shapes,
        in_specs=[VMEM] * 2,
        out_specs=[VMEM] * len(shapes),
        compiler_params=limit(6),
        name="halve",
    )(held, got)


def join_kernel(first, second, out):
    rows = first.shape[0]
    out[:rows, :] = first[...]
    out[rows:, :] = second[...]


def join(first, second):
    return pl.pallas_call(
        join_kernel,
        out_shape=jax.ShapeDtypeStruct((2 * first.shape[0], HD), bf16),
        in_specs=[VMEM] * 2,
        out_specs=VMEM,
        compiler_params=limit(4),
        name="join",
    )(first, second)


def place_weight_kernel(own_low, own_high, oth_low, oth_high, out, sems):
    core = lax.rem(lax.axis_index("seq"), 2)
    rows = own_low.shape[0] // 4
    pairs = []
    for halves, side in (((own_low, own_high), core), ((oth_low, oth_high), 1 - core)):
        code = chip_code(side)
        cols = pl.ds(pl.multiple_of(side * HD, HD), HD)
        for index in range(8):
            source = halves[index // 4].at[pl.ds(index % 4 * rows, rows)]
            at = pl.ds(pl.multiple_of((index ^ code) * rows, 16), rows)
            pairs.append((source, out.at[at, cols]))
    for copy in run_copies(pairs, sems):
        copy.wait()


def place_weight(*pieces):
    return pl.pallas_call(
        place_weight_kernel,
        out_shape=jax.ShapeDtypeStruct((2 * pieces[0].shape[0], KVH * HD), bf16),
        in_specs=[ANY] * 4,
        out_specs=ANY,
        scratch_shapes=[pltpu.SemaphoreType.DMA((16,))],
        compiler_params=limit(2),
        name="place_weight",
    )(*pieces)


def place_tokens_kernel(q_own, q_oth, k_own, k_oth, q_out, k_out, sems):
    core = lax.rem(lax.axis_index("seq"), 2)
    pairs = []
    for own, oth, out in ((q_own, q_oth, q_out), (k_own, k_oth, k_out)):
        width = own.shape[1]
        for source, side in ((own, core), (oth, 1 - core)):
            cols = pl.ds(pl.multiple_of(side * width, HD), width)
            pairs.append((source, out.at[:, cols]))
    for copy in run_copies(pairs, sems):
        copy.wait()


def place_tokens(q_own, q_oth, k_own, k_oth):
    return pl.pallas_call(
        place_tokens_kernel,
        out_shape=[
            jax.ShapeDtypeStruct((own.shape[0], 2 * own.shape[1]), bf16) for own in (q_own, k_own)
        ],
        in_specs=[ANY] * 4,
        out_specs=[ANY] * 2,
        scratch_shapes=[pltpu.SemaphoreType.DMA((4,))],
        compiler_params=limit(2),
        name="place_tokens",
    )(q_own, q_oth, k_own, k_oth)


def reduce_any(spiked, value_grad, core, place, row):
    n_dp, n_seq = lax.axis_size("dp"), lax.axis_size("seq")
    chip = place // 2
    part = lax.dot_general(
        spiked, value_grad, (((0,), (0,)), ((), ())), preferred_element_type=f32
    )
    steps = [("dp", 1 << b, (row >> b) & 1) for b in range(n_dp.bit_length() - 2, -1, -1)]
    chip_steps = [
        ("seq", 2 << b, (chip >> b) & 1) for b in range((n_seq // 2).bit_length() - 1)
    ]
    for axis, flip, bit in steps + chip_steps:
        half = part.shape[0] // 2
        send = lax.dynamic_slice_in_dim(part, (1 - bit) * half, half, 0).astype(bf16)
        keep = lax.dynamic_slice_in_dim(part, bit * half, half, 0)
        part = keep + swapped(send, axis, flip).astype(f32)
    owned = part.astype(bf16)
    for axis, flip, bit in chip_steps[::-1]:
        owned = ordered(bit, owned, swapped(owned, axis, flip))
    return ordered(core, owned, swapped(owned, "seq", 1), axis=1)


def after(value, *others):
    return lax.optimization_barrier((value, *others))[0]


def body(hidden_in, spike_level, value_weight, queries, key_states, spike_mask, out_grad):
    tok = hidden_in.shape[1]
    n_dp, n_seq = lax.axis_size("dp"), lax.axis_size("seq")
    place, row = lax.axis_index("seq"), lax.axis_index("dp")
    core = place % 2
    assert 0 < WINDOW - 2 * tok <= tok and 2 * tok % BLOCK == 0

    def both(value):
        return value, swapped(value, "seq", 1)

    own_keys = key_states[0]
    near_keys, far_keys = lax.optimization_barrier((shifted(own_keys, 2), shifted(own_keys, 4)))
    query_own, query_out, grad_own, grad_out, marks = split(
        tok, queries[0], out_grad[0], jnp.transpose(spike_mask, (2, 0, 1)), spike_level
    )
    near_keys, far_keys, _ = lax.optimization_barrier((near_keys, far_keys, query_out))
    keys, keys_out = pack(tok, own_keys, near_keys, far_keys)
    weight_half = lax.dynamic_slice_in_dim(value_weight, core * HD, HD, 1)
    raw = [query_own, swapped(query_out, "seq", 1), grad_own, swapped(grad_out, "seq", 1)]
    raw += [keys, swapped(keys_out, "seq", 1)]
    marks = both(marks)
    if n_dp == 2:
        weight = (weight_half, swapped(weight_half, "dp", 1))
    else:
        weight = (lax.all_gather(weight_half, "dp", axis=0, tiled=True),)

    own, near, far, top, norm = value_terms(tok, raw, marks)
    near, far = shifted(near, -2), shifted(far, -4)
    values, tail, spiked = project(tok, both(after(hidden_in[0], keys_out)), marks, weight)

    fast = n_dp == 2 and n_seq == 16 and hidden_in.shape[2] % 256 == 0
    if fast:
        keep, send = weight_terms(tok, spiked, (own, near, far))
        values, tail = lax.optimization_barrier((values, tail, send))[:2]
        got = crossed(send, (n_seq, n_seq))
    window = (values, shifted(values, 2), shifted(tail, 4))
    own_k, near_k, far_k, query_mine, query_send = key_terms(tok, raw, top, norm, window)
    if fast:
        keep, send = halve(keep, after(got, own_k))
        near_k, far_k = lax.optimization_barrier((near_k, far_k, send))[:2]
        got = crossed(send, (2, 4))
    near_k, far_k = shifted(near_k, -2), shifted(far_k, -4)
    if fast:
        keep, send = halve(keep, got)
        query_send = after(query_send, send)
        got = crossed(send, (4, 2))
    query_got = swapped(query_send, "seq", 1)
    if fast:
        keep, send = halve(keep, after(got, near_k, far_k, query_got))
        near_k, far_k = lax.optimization_barrier((near_k, far_k, send))[:2]
        got = crossed(send, (8, 8))
    key_mine, key_send = sum_keys(tok, own_k, near_k, far_k)
    key_got = swapped(key_send, "seq", 1)
    if fast:
        (owned,) = halve(keep, after(got, key_got), last=True)
        key_got = after(key_got, owned)
        got = crossed(owned, (8, 8))
    query_grad, key_grad = place_tokens(query_mine, query_got, key_mine, key_got)
    if fast:
        owned = join(owned, after(got, query_grad))
        owned = join(owned, crossed(owned, (4, 2)))
        other = crossed(owned, (2, 4))
        weight_grad = place_weight(
            owned, other, swapped(owned, "seq", 1), swapped(other, "seq", 1)
        )
    else:
        value_grad = value_sum(tok, own, near, far).astype(bf16)
        weight_grad = reduce_any(spiked, value_grad, core, place, row)
    return (query_grad[None], key_grad[None], weight_grad)


def solution(mesh):
    placed = (
        P("dp", "seq", None),
        P("dp", "seq"),
        P("dp", None),
        P("dp", "seq", None),
        P("dp", "seq", None),
        P("dp", "seq", None),
        P("dp", "seq", None),
    )
    return jax.shard_map(
        body,
        mesh=mesh,
        in_specs=placed,
        out_specs=(P("dp", "seq", None), P("dp", "seq", None), P("dp", None)),
        check_vma=False,
    )
```

```python
import functools
import math

import jax
import jax.numpy as jnp
from jax import lax
from jax.experimental import pallas as pl
from jax.experimental.pallas import tpu as pltpu
from jax.sharding import PartitionSpec as P

QH = 14
KVH = 2
HD = 128
WINDOW = 512
LEVELS = 4
GROUP = 7
BLOCK = 128
SPAN = WINDOW + BLOCK

masked_score = -1e30
score_scale = 1.0 / math.sqrt(HD)
exp2_scale = score_scale * math.log2(math.e)

bf16 = jnp.bfloat16
f32 = jnp.float32
ANY = pl.BlockSpec(memory_space=pltpu.HBM)
VMEM = pl.BlockSpec(memory_space=pltpu.VMEM)


def limit(mib):
    return pltpu.CompilerParams(vmem_limit_bytes=mib * 1024 * 1024)


def shifted(value, steps, cores=(0, 1)):
    count = lax.axis_size("seq")
    pairs = [(i, (i + steps) % count) for i in range(count) if i % 2 in cores]
    return lax.ppermute(value, "seq", pairs)


def swapped(value, axis, flip):
    return lax.ppermute(value, axis, [(i, i ^ flip) for i in range(lax.axis_size(axis))])


def crossed(value, flip):
    count = lax.axis_size("dp") * lax.axis_size("seq")
    return lax.ppermute(value, ("dp", "seq"), [(i, i ^ flip) for i in range(count)])


def ordered(bit, own, other, axis=0):
    return jnp.where(
        bit == 0,
        jnp.concatenate([own, other], axis=axis),
        jnp.concatenate([other, own], axis=axis),
    )


def run_copies(pairs, sems):
    copies = [pltpu.make_async_copy(src, dst, sems.at[n]) for n, (src, dst) in enumerate(pairs)]
    for copy in copies:
        copy.start()
    return copies


def split_kernel(
    tok, q_ref, g_ref, m_ref, l_ref, w_ref, k_ref, *rest
):
    q_own, q_send, g_own, g_send, marks, w_half, k_tail, m_buf, l_buf, sems = rest
    core = lax.rem(lax.axis_index("seq"), 2)
    wide = GROUP * HD
    slim = pl.ds(pl.multiple_of(core * HD, HD), HD)
    pairs = [(m_ref, m_buf), (l_ref, l_buf), (w_ref.at[:, slim], w_half)]
    tail = k_tail.shape[0]
    pairs.append((k_ref.at[pl.ds(tok - tail, tail)], k_tail))
    for source, own, send in ((q_ref, q_own, q_send), (g_ref, g_own, g_send)):
        for target, side in ((own, core), (send, 1 - core)):
            pairs.append((source.at[:, pl.ds(pl.multiple_of(side * wide, HD), wide)], target))
    copies = run_copies(pairs, sems)
    for copy in copies:
        copy.wait()
    for head in range(QH):
        marks[head : head + 1, :] = m_buf[head]
    marks[QH : QH + 1, :] = l_buf[...]


def in_hbm(value):
    return pltpu.with_memory_space_constraint(value, pltpu.HBM)


def split(tok, *values):
    weight_rows = values[4].shape[0]
    half = jax.ShapeDtypeStruct((tok, GROUP * HD), bf16)
    return pl.pallas_call(
        functools.partial(split_kernel, tok),
        out_shape=[half] * 4
        + [
            jax.ShapeDtypeStruct((QH + 1, tok), jnp.int32),
            jax.ShapeDtypeStruct((weight_rows, HD), bf16),
            jax.ShapeDtypeStruct((WINDOW - 2 * tok, KVH * HD), bf16),
        ],
        in_specs=[ANY] * 6,
        out_specs=[VMEM] * 7,
        scratch_shapes=[
            pltpu.VMEM((QH, 1, tok), jnp.int32),
            pltpu.VMEM((1, tok), jnp.int32),
            pltpu.SemaphoreType.DMA((8,)),
        ],
        compiler_params=limit(6),
        name="split",
    )(*[in_hbm(value) for value in values])


def pack_kernel(tok, own, near, far, mine, send, sems):
    core = lax.rem(lax.axis_index("seq"), 2)
    rest = WINDOW - 2 * tok
    sides = ((mine, core), (send, 1 - core))
    pairs = []
    for target, side in sides:
        cols = pl.ds(pl.multiple_of(side * HD, HD), HD)
        pairs.append((own.at[:, cols], target.at[pl.ds(rest + tok, tok)]))
    copies = run_copies(pairs, sems)
    for target, side in sides:
        cols = pl.ds(pl.multiple_of(side * HD, HD), HD)
        target[:rest, :] = far[:, cols]
        target[rest : rest + tok, :] = near[:, cols]
    for copy in copies:
        copy.wait()


def pack(tok, own, near, far):
    half = jax.ShapeDtypeStruct((WINDOW, HD), bf16)
    return pl.pallas_call(
        functools.partial(pack_kernel, tok),
        out_shape=[half] * 2,
        in_specs=[ANY] + [VMEM] * 2,
        out_specs=[VMEM] * 2,
        scratch_shapes=[pltpu.SemaphoreType.DMA((2,))],
        compiler_params=limit(4),
        name="pack",
    )(in_hbm(own), near, far)


def lay_out(core, tok, raw, q_buf, g_buf, k_buf):
    q_own, q_oth, g_own, g_oth, k_own, k_oth = raw
    rest = WINDOW - 2 * tok
    for own, oth, buf, first, begin in (
        (k_own, k_oth, k_buf, rest, rest),
        (k_own, k_oth, k_buf, rest + tok, WINDOW),
        (q_own, q_oth, q_buf, 0, 0),
        (g_own, g_oth, g_buf, 0, 0),
    ):
        buf[pl.ds(pl.multiple_of(begin + core * tok, 64), tok), :] = own[first : first + tok, :]
        buf[pl.ds(pl.multiple_of(begin + (1 - core) * tok, 64), tok), :] = oth[
            first : first + tok, :
        ]
    k_buf[:rest, :] = jnp.where(core == 1, k_own[:rest, :], k_oth[:rest, :])


def head_masks(core, own, oth):
    spikes = jnp.where(
        core == 0,
        jnp.concatenate([own, oth], axis=1),
        jnp.concatenate([oth, own], axis=1),
    ).astype(f32)
    return jnp.where(core == 0, spikes[:GROUP], spikes[GROUP:])


def biases(chip, tok, block):
    later = lax.broadcasted_iota(jnp.int32, (BLOCK, BLOCK), 0)
    query = lax.broadcasted_iota(jnp.int32, (BLOCK, BLOCK), 1)
    first_key = WINDOW - chip * 2 * tok
    tiles = SPAN // BLOCK
    result = []
    for tile in range(tiles):
        begin = (block + tile) * BLOCK
        bias = None
        if begin < WINDOW:
            bias = jnp.where(begin >= first_key, 0.0, masked_score).astype(f32)
        if tile == 0:
            bias = jnp.where(later > query, bias if bias is not None else 0.0, masked_score)
        elif tile == tiles - 1:
            bias = jnp.where(later <= query, 0.0, masked_score)
        result.append(bias)
    return result


def dot_nt(a, b):
    return lax.dot_general(a, b, (((1,), (1,)), ((), ())), preferred_element_type=f32)


def dot_tn(a, b):
    return lax.dot_general(a, b, (((0,), (0,)), ((), ())), preferred_element_type=f32)


def masked(scores, bias):
    tiles = [scores[n * BLOCK : (n + 1) * BLOCK] for n in range(len(bias))]
    return jnp.concatenate(
        [tile if add is None else tile + add for tile, add in zip(tiles, bias)], axis=0
    )


def stacked(buf, block):
    rows = slice(block * BLOCK, (block + 1) * BLOCK)
    return jnp.concatenate(
        [buf[rows, head * HD : (head + 1) * HD] for head in range(GROUP)], axis=0
    )


def value_kernel(tok, *refs):
    raw, m_own, m_oth = refs[:6], *refs[6:8]
    own_out, near_out, far_out, top_out, norm_out = refs[8:13]
    q_buf, g_buf, k_buf, p_buf, acc = refs[13:]
    place = lax.axis_index("seq")
    core, chip = lax.rem(place, 2), lax.div(place, 2)
    lay_out(core, tok, raw, q_buf, g_buf, k_buf)
    spikes = head_masks(core, m_own[:QH, :], m_oth[:QH, :])
    acc[...] = jnp.zeros_like(acc)
    for block in range(2 * tok // BLOCK):
        bias = biases(chip, tok, block)
        begin = block * BLOCK
        rows = slice(begin, begin + BLOCK)
        keys = k_buf[begin : begin + SPAN, :]
        for head in range(GROUP):
            cols = slice(head * HD, (head + 1) * HD)
            scores = masked(dot_nt(keys, q_buf[rows, cols]), bias)
            top = jnp.max(scores, axis=0, keepdims=True)
            expo = jnp.exp2((scores - top) * exp2_scale)
            norm = spikes[head : head + 1, rows] / jnp.sum(expo, axis=0, keepdims=True)
            p_buf[:, cols] = (expo * norm).astype(bf16)
            at = block * GROUP + head
            top_out[at : at + 1, :] = top
            norm_out[at : at + 1, :] = norm
        acc[begin : begin + SPAN, :] += jnp.dot(
            p_buf[...], stacked(g_buf, block), preferred_element_type=f32
        )
    rest = WINDOW - 2 * tok
    far_out[...] = acc[:rest, :].astype(bf16)
    near_out[...] = acc[rest:WINDOW, :].astype(bf16)
    own_out[...] = acc[WINDOW:, :]


def key_kernel(tok, *refs):
    raw = refs[:6]
    top_in, norm_in, v_own, v_near, v_far = refs[6:11]
    own_out, near_out, far_out, mine_out, send_out = refs[11:16]
    q_buf, g_buf, k_buf, v_buf, d_buf, acc, r_buf = refs[16:]
    place = lax.axis_index("seq")
    core, chip = lax.rem(place, 2), lax.div(place, 2)
    rest = WINDOW - 2 * tok
    lay_out(core, tok, raw, q_buf, g_buf, k_buf)
    v_buf[:rest, :] = v_far[...]
    v_buf[rest:WINDOW, :] = v_near[...]
    v_buf[WINDOW:, :] = v_own[...]
    acc[...] = jnp.zeros_like(acc)
    for block in range(2 * tok // BLOCK):
        bias = biases(chip, tok, block)
        begin = block * BLOCK
        rows = slice(begin, begin + BLOCK)
        keys = k_buf[begin : begin + SPAN, :]
        values = v_buf[begin : begin + SPAN, :]
        for head in range(GROUP):
            cols = slice(head * HD, (head + 1) * HD)
            at = block * GROUP + head
            scores = masked(dot_nt(keys, q_buf[rows, cols]), bias)
            probs = jnp.exp2((scores - top_in[at : at + 1, :]) * exp2_scale)
            probs = probs * norm_in[at : at + 1, :]
            prob_grad = dot_nt(values, g_buf[rows, cols])
            delta = jnp.sum(probs.astype(bf16).astype(f32) * prob_grad, axis=0, keepdims=True)
            d_buf[:, cols] = (probs * (prob_grad - delta)).astype(bf16)
        acc[begin : begin + SPAN, :] += jnp.dot(
            d_buf[...], stacked(q_buf, block), preferred_element_type=f32
        )
        query_part = dot_tn(d_buf[...], keys) * score_scale
        for head in range(GROUP):
            cols = slice(head * HD, (head + 1) * HD)
            r_buf[rows, cols] = query_part[head * BLOCK : (head + 1) * BLOCK].astype(bf16)
    mine_out[...] = r_buf[pl.ds(pl.multiple_of(core * tok, 64), tok), :]
    send_out[...] = r_buf[pl.ds(pl.multiple_of((1 - core) * tok, 64), tok), :]
    far_out[...] = (acc[:rest, :] * score_scale).astype(bf16)
    near_out[...] = (acc[rest:WINDOW, :] * score_scale).astype(bf16)
    own_out[...] = acc[WINDOW:, :] * score_scale


def head_scratch(tok):
    return [
        pltpu.VMEM((2 * tok, GROUP * HD), bf16),
        pltpu.VMEM((2 * tok, GROUP * HD), bf16),
        pltpu.VMEM((WINDOW + 2 * tok, HD), bf16),
    ]


def term_shapes(tok):
    return [
        jax.ShapeDtypeStruct((2 * tok, HD), f32),
        jax.ShapeDtypeStruct((2 * tok, HD), bf16),
        jax.ShapeDtypeStruct((WINDOW - 2 * tok, HD), bf16),
    ]


def value_terms(tok, raw, spikes):
    stats = jax.ShapeDtypeStruct((2 * tok // BLOCK * GROUP, BLOCK), f32)
    return pl.pallas_call(
        functools.partial(value_kernel, tok),
        out_shape=term_shapes(tok) + [stats, stats],
        in_specs=[VMEM] * 8,
        out_specs=[VMEM] * 5,
        scratch_shapes=head_scratch(tok)
        + [
            pltpu.VMEM((SPAN, GROUP * HD), bf16),
            pltpu.VMEM((WINDOW + 2 * tok, HD), f32),
        ],
        compiler_params=limit(12),
        name="value_terms",
    )(*raw, *spikes)


def key_terms(tok, raw, top, norm, values):
    half = jax.ShapeDtypeStruct((tok, GROUP * HD), bf16)
    return pl.pallas_call(
        functools.partial(key_kernel, tok),
        out_shape=term_shapes(tok) + [half, half],
        in_specs=[VMEM] * 11,
        out_specs=[VMEM] * 5,
        scratch_shapes=head_scratch(tok)
        + [
            pltpu.VMEM((WINDOW + 2 * tok, HD), bf16),
            pltpu.VMEM((SPAN, GROUP * HD), bf16),
            pltpu.VMEM((WINDOW + 2 * tok, HD), f32),
            pltpu.VMEM((2 * tok, GROUP * HD), bf16),
        ],
        compiler_params=limit(14),
        name="key_terms",
    )(*raw, top, norm, *values)


def sum_keys_kernel(tok, own, near, far, mine, send, buf):
    core = lax.rem(lax.axis_index("seq"), 2)
    buf[...] = value_sum(tok, own[...], near[...], far[...])
    mine[...] = buf[pl.ds(pl.multiple_of(core * tok, 64), tok), :].astype(bf16)
    send[...] = buf[pl.ds(pl.multiple_of((1 - core) * tok, 64), tok), :].astype(bf16)


def sum_keys(tok, own, near, far):
    half = jax.ShapeDtypeStruct((tok, HD), bf16)
    return pl.pallas_call(
        functools.partial(sum_keys_kernel, tok),
        out_shape=[half, half],
        in_specs=[VMEM] * 3,
        out_specs=[VMEM] * 2,
        scratch_shapes=[pltpu.VMEM((2 * tok, HD), f32)],
        compiler_params=limit(4),
        name="sum_keys",
    )(own, near, far)


def column(row):
    size = row.shape[1]
    diagonal = lax.broadcasted_iota(jnp.int32, (size, size), 0) == lax.broadcasted_iota(
        jnp.int32, (size, size), 1
    )
    return jnp.sum(jnp.where(diagonal, row, 0.0), axis=1, keepdims=True)


def project_kernel(tok, split, h_own, h_oth, l_own, l_oth, w_own, w_oth, out, tail, spiked, w_buf, sems):
    core = lax.rem(lax.axis_index("seq"), 2)
    if split:
        row = lax.axis_index("dp")
        depth = w_own.shape[0]
        pairs = [
            (w_own, w_buf.at[pl.ds(pl.multiple_of(row * depth, depth), depth)]),
            (w_oth, w_buf.at[pl.ds(pl.multiple_of((1 - row) * depth, depth), depth)]),
        ]
    else:
        pairs = [(w_own, w_buf)]
    copies = run_copies(pairs, sems)
    for source, level, place in ((h_own, l_own, core), (h_oth, l_oth, 1 - core)):
        factor = column(level[QH : QH + 1, :].astype(f32) / LEVELS)
        rows = pl.ds(pl.multiple_of(place * tok, 64), tok)
        spiked[rows, :] = (source[...].astype(f32) * factor).astype(bf16)
    for copy in copies:
        copy.wait()
    values = jnp.dot(spiked[...], w_buf[...], preferred_element_type=f32).astype(bf16)
    out[...] = values
    tail[...] = values[4 * tok - WINDOW :, :]


def project(tok, hidden, levels, weight):
    depth = hidden[0].shape[1]
    split = len(weight) == 2
    return pl.pallas_call(
        functools.partial(project_kernel, tok, split),
        out_shape=[
            jax.ShapeDtypeStruct((2 * tok, HD), bf16),
            jax.ShapeDtypeStruct((WINDOW - 2 * tok, HD), bf16),
            jax.ShapeDtypeStruct((2 * tok, depth), bf16),
        ],
        in_specs=[VMEM] * 4 + [ANY] * 2,
        out_specs=[VMEM] * 3,
        scratch_shapes=[pltpu.VMEM((depth, HD), bf16), pltpu.SemaphoreType.DMA((2,))],
        compiler_params=limit(14),
        name="project",
    )(*hidden, *levels, weight[0], weight[-1])


def value_sum(tok, own, near, far):
    late = own[4 * tok - WINDOW :] + far.astype(f32)
    early = own[: 4 * tok - WINDOW]
    return jnp.concatenate([early, late], axis=0) + near.astype(f32)


def weight_kernel(tok, spiked, own, near, far, keep, send, w_buf):
    rows = spiked.shape[1] // 16
    value_grad = value_sum(tok, own[...], near[...], far[...]).astype(bf16)
    mine = block_code()
    for part in range(4):
        term = dot_tn(spiked[:, part * 4 * rows : (part + 1) * 4 * rows], value_grad)
        for piece in range(4):
            at = (part * 4 + piece) ^ mine
            w_buf[pl.ds(pl.multiple_of(at * rows, 16), rows), :] = term[
                piece * rows : (piece + 1) * rows
            ]
    keep[...] = w_buf[: 8 * rows, :]
    send[...] = w_buf[8 * rows :, :].astype(bf16)


def chip_bits():
    chip = lax.div(lax.axis_index("seq"), 2)
    return chip & 1, (chip >> 1) & 1, (chip >> 2) & 1


def block_code():
    return lax.axis_index("dp") * 8 + chip_code()


def chip_code():
    y, near, far = chip_bits()
    return y * 4 + near * 2 + far


def weight_terms(tok, spiked, terms):
    depth = spiked.shape[1]
    return pl.pallas_call(
        functools.partial(weight_kernel, tok),
        out_shape=[
            jax.ShapeDtypeStruct((depth // 2, HD), f32),
            jax.ShapeDtypeStruct((depth // 2, HD), bf16),
        ],
        in_specs=[VMEM] * 4,
        out_specs=[VMEM] * 2,
        scratch_shapes=[pltpu.VMEM((depth, HD), f32)],
        compiler_params=limit(14),
        name="weight_terms",
    )(spiked, *terms)


def reduce_kernel(count, held, *refs):
    total = held[...]
    for got in refs[:count]:
        total = total + got[...].astype(f32)
    outs = refs[count:]
    rows = total.shape[0] // len(outs)
    outs[0][...] = total[:rows].astype(outs[0].dtype)
    for part in range(1, len(outs)):
        outs[part][...] = total[part * rows : (part + 1) * rows].astype(bf16)


def reduce_step(held, got, parts):
    rows = held.shape[0] // parts
    shapes = [jax.ShapeDtypeStruct((rows, HD), bf16)] * parts
    if parts > 1:
        shapes[0] = jax.ShapeDtypeStruct((rows, HD), f32)
    return pl.pallas_call(
        functools.partial(reduce_kernel, len(got)),
        out_shape=shapes,
        in_specs=[VMEM] * (1 + len(got)),
        out_specs=[VMEM] * parts,
        compiler_params=limit(6),
        name="reduce_step",
    )(held, *got)


def join_kernel(first, second, out):
    rows = first.shape[0]
    out[:rows, :] = first[...]
    out[rows:, :] = second[...]


def join(first, second):
    return pl.pallas_call(
        join_kernel,
        out_shape=jax.ShapeDtypeStruct((2 * first.shape[0], HD), bf16),
        in_specs=[VMEM] * 2,
        out_specs=VMEM,
        compiler_params=limit(4),
        name="join",
    )(first, second)


def place_weight_kernel(*refs):
    out, sems = refs[8:]
    core = lax.rem(lax.axis_index("seq"), 2)
    code = chip_code()
    rows = refs[0].shape[0] // 2
    pairs = []
    for pieces, side in ((refs[:4], core), (refs[4:8], 1 - core)):
        cols = pl.ds(pl.multiple_of(side * HD, HD), HD)
        for index in range(8):
            source = pieces[index // 2].at[pl.ds(index % 2 * rows, rows)]
            at = pl.ds(pl.multiple_of((index ^ code) * rows, 16), rows)
            pairs.append((source, out.at[at, cols]))
    for copy in run_copies(pairs, sems):
        copy.wait()


def place_weight(*pieces):
    return pl.pallas_call(
        place_weight_kernel,
        out_shape=jax.ShapeDtypeStruct((4 * pieces[0].shape[0], KVH * HD), bf16),
        in_specs=[ANY] * 8,
        out_specs=ANY,
        scratch_shapes=[pltpu.SemaphoreType.DMA((16,))],
        compiler_params=limit(2),
        name="place_weight",
    )(*pieces)


def place_tokens_kernel(q_own, q_oth, k_own, k_oth, q_out, k_out, sems):
    core = lax.rem(lax.axis_index("seq"), 2)
    pairs = []
    for own, oth, out in ((q_own, q_oth, q_out), (k_own, k_oth, k_out)):
        width = own.shape[1]
        for source, side in ((own, core), (oth, 1 - core)):
            cols = pl.ds(pl.multiple_of(side * width, HD), width)
            pairs.append((source, out.at[:, cols]))
    for copy in run_copies(pairs, sems):
        copy.wait()


def place_tokens(q_own, q_oth, k_own, k_oth):
    return pl.pallas_call(
        place_tokens_kernel,
        out_shape=[
            jax.ShapeDtypeStruct((own.shape[0], 2 * own.shape[1]), bf16) for own in (q_own, k_own)
        ],
        in_specs=[ANY] * 4,
        out_specs=[ANY] * 2,
        scratch_shapes=[pltpu.SemaphoreType.DMA((4,))],
        compiler_params=limit(2),
        name="place_tokens",
    )(q_own, q_oth, k_own, k_oth)


def reduce_any(spiked, value_grad):
    n_dp, n_seq = lax.axis_size("dp"), lax.axis_size("seq")
    place, row = lax.axis_index("seq"), lax.axis_index("dp")
    core, chip = place % 2, place // 2
    part = lax.dot_general(
        spiked, value_grad, (((0,), (0,)), ((), ())), preferred_element_type=f32
    )
    steps = [("dp", 1 << b, (row >> b) & 1) for b in range(n_dp.bit_length() - 2, -1, -1)]
    chip_steps = [
        ("seq", 2 << b, (chip >> b) & 1) for b in range((n_seq // 2).bit_length() - 1)
    ]
    for axis, flip, bit in steps + chip_steps:
        half = part.shape[0] // 2
        send = lax.dynamic_slice_in_dim(part, (1 - bit) * half, half, 0).astype(bf16)
        keep = lax.dynamic_slice_in_dim(part, bit * half, half, 0)
        part = keep + swapped(send, axis, flip).astype(f32)
    owned = part.astype(bf16)
    for axis, flip, bit in chip_steps[::-1]:
        owned = ordered(bit, owned, swapped(owned, axis, flip))
    return ordered(core, owned, swapped(owned, "seq", 1), axis=1)


def body(hidden_in, spike_level, value_weight, queries, key_states, spike_mask, out_grad):
    tok = hidden_in.shape[1]
    n_dp, n_seq = lax.axis_size("dp"), lax.axis_size("seq")
    assert 0 < WINDOW - 2 * tok <= tok and 2 * tok % BLOCK == 0

    def both(value):
        return value, swapped(value, "seq", 1)

    own_keys = key_states[0]
    query_own, query_out, grad_own, grad_out, marks_own, weight_half, key_tail = split(
        tok,
        queries[0],
        out_grad[0],
        jnp.transpose(spike_mask, (2, 0, 1)),
        spike_level,
        value_weight,
        own_keys,
    )
    near_keys, far_keys = lax.optimization_barrier(
        (shifted(own_keys, 2), shifted(key_tail, 4, cores=(1,)))
    )
    query_oth, grad_oth, marks_oth = (
        swapped(value, "seq", 1) for value in (query_out, grad_out, marks_own)
    )
    near_keys, far_keys, query_oth, grad_oth, marks_oth = lax.optimization_barrier(
        (near_keys, far_keys, query_oth, grad_oth, marks_oth)
    )
    keys_own, keys_out = pack(tok, own_keys, near_keys, far_keys)
    if n_dp == 2:
        weight = (weight_half, swapped(weight_half, "dp", 1))
    else:
        weight = (lax.all_gather(weight_half, "dp", axis=0, tiled=True),)
    keys_oth, hidden_own, *weight = lax.optimization_barrier(
        (swapped(keys_out, "seq", 1), hidden_in[0], *weight)
    )
    raw = [query_own, query_oth, grad_own, grad_oth, keys_own, keys_oth]
    marks = (marks_own, marks_oth)

    own, near, far, top, norm = value_terms(tok, raw, marks)
    near, far = shifted(near, -2), shifted(far, -4)
    values, tail, spiked = project(tok, both(hidden_own), marks, weight)

    fast = n_dp == 2 and n_seq == 16 and hidden_in.shape[2] % 256 == 0
    if fast:
        keep, send = weight_terms(tok, spiked, (own, near, far))
        values, tail, send = lax.optimization_barrier((values, tail, send))
        got = crossed(send, n_seq)
    window = (values, shifted(values, 2), shifted(tail, 4))
    own_k, near_k, far_k, query_mine, query_out = key_terms(tok, raw, top, norm, window)
    if fast:
        got, own_k = lax.optimization_barrier((got, own_k))
        keep, *sends = reduce_step(keep, [got], 4)
        near_k, far_k, *sends = lax.optimization_barrier((near_k, far_k, *sends))
        got = [crossed(send, flip) for send, flip in zip(sends, (4, 2, 6))]
    near_k, far_k = shifted(near_k, -2), shifted(far_k, -4)
    if fast:
        keep, send = reduce_step(keep, got, 2)
        query_out, send = lax.optimization_barrier((query_out, send))
        got = crossed(send, 8)
    query_got = swapped(query_out, "seq", 1)
    if fast:
        got, near_k, far_k, query_got = lax.optimization_barrier((got, near_k, far_k, query_got))
        (owned,) = reduce_step(keep, [got], 1)
        near_k, owned = lax.optimization_barrier((near_k, owned))
    key_mine, key_out = sum_keys(tok, own_k, near_k, far_k)
    key_got = swapped(key_out, "seq", 1)
    if fast:
        got, key_got = lax.optimization_barrier((crossed(owned, 8), key_got))
        owned = join(owned, got)
        key_got, owned = lax.optimization_barrier((key_got, owned))
    query_grad, key_grad = place_tokens(query_mine, query_got, key_mine, key_got)
    if fast:
        pieces = [crossed(owned, flip) for flip in (4, 2, 6)]
        *pieces, key_grad = lax.optimization_barrier((*pieces, key_grad))
        pieces = [owned, *pieces]
        weight_grad = place_weight(*pieces, *[swapped(piece, "seq", 1) for piece in pieces])
    else:
        value_grad = value_sum(tok, own, near, far).astype(bf16)
        weight_grad = reduce_any(spiked, value_grad)
    return (query_grad[None], key_grad[None], weight_grad)


def solution(mesh):
    placed = (
        P("dp", "seq", None),
        P("dp", "seq"),
        P("dp", None),
        P("dp", "seq", None),
        P("dp", "seq", None),
        P("dp", "seq", None),
        P("dp", "seq", None),
    )
    return jax.shard_map(
        body,
        mesh=mesh,
        in_specs=placed,
        out_specs=(P("dp", "seq", None), P("dp", "seq", None), P("dp", None)),
        check_vma=False,
    )
```

```python
import functools
import math

import jax
import jax.numpy as jnp
from jax import lax
from jax.experimental import pallas as pl
from jax.experimental.pallas import tpu as pltpu
from jax.sharding import PartitionSpec as P

QH = 14
KVH = 2
HD = 128
WINDOW = 512
LEVELS = 4
GROUP = 7
BLOCK = 128
SPAN = WINDOW + BLOCK

masked_score = -1e30
score_scale = 1.0 / math.sqrt(HD)
exp2_scale = score_scale * math.log2(math.e)

bf16 = jnp.bfloat16
f32 = jnp.float32
ANY = pl.BlockSpec(memory_space=pltpu.HBM)
VMEM = pl.BlockSpec(memory_space=pltpu.VMEM)


def limit(mib):
    return pltpu.CompilerParams(vmem_limit_bytes=mib * 1024 * 1024)


def shifted(value, steps, cores=(0, 1)):
    count = lax.axis_size("seq")
    pairs = [(i, (i + steps) % count) for i in range(count) if i % 2 in cores]
    return lax.ppermute(value, "seq", pairs)


def swapped(value, axis, flip):
    return lax.ppermute(value, axis, [(i, i ^ flip) for i in range(lax.axis_size(axis))])


def crossed(value, flip):
    count = lax.axis_size("dp") * lax.axis_size("seq")
    return lax.ppermute(value, ("dp", "seq"), [(i, i ^ flip) for i in range(count)])


def ordered(bit, own, other, axis=0):
    return jnp.where(
        bit == 0,
        jnp.concatenate([own, other], axis=axis),
        jnp.concatenate([other, own], axis=axis),
    )


def run_copies(pairs, sems):
    copies = [pltpu.make_async_copy(src, dst, sems.at[n]) for n, (src, dst) in enumerate(pairs)]
    for copy in copies:
        copy.start()
    return copies


def split_kernel(
    tok, q_ref, g_ref, m_ref, l_ref, w_ref, k_ref, *rest
):
    q_own, q_send, g_own, g_send, marks, w_half, k_tail, m_buf, l_buf, sems = rest
    core = lax.rem(lax.axis_index("seq"), 2)
    wide = GROUP * HD
    slim = pl.ds(pl.multiple_of(core * HD, HD), HD)
    pairs = [(m_ref, m_buf), (l_ref, l_buf), (w_ref.at[:, slim], w_half)]
    tail = k_tail.shape[0]
    pairs.append((k_ref.at[pl.ds(tok - tail, tail)], k_tail))
    for source, own, send in ((q_ref, q_own, q_send), (g_ref, g_own, g_send)):
        for target, side in ((own, core), (send, 1 - core)):
            pairs.append((source.at[:, pl.ds(pl.multiple_of(side * wide, HD), wide)], target))
    copies = run_copies(pairs, sems)
    for copy in copies:
        copy.wait()
    for head in range(QH):
        marks[head : head + 1, :] = m_buf[head]
    marks[QH : QH + 1, :] = l_buf[...]


def in_hbm(value):
    return pltpu.with_memory_space_constraint(value, pltpu.HBM)


def split(tok, *values):
    weight_rows = values[4].shape[0]
    half = jax.ShapeDtypeStruct((tok, GROUP * HD), bf16)
    return pl.pallas_call(
        functools.partial(split_kernel, tok),
        out_shape=[half] * 4
        + [
            jax.ShapeDtypeStruct((QH + 1, tok), jnp.int32),
            jax.ShapeDtypeStruct((weight_rows, HD), bf16),
            jax.ShapeDtypeStruct((WINDOW - 2 * tok, KVH * HD), bf16),
        ],
        in_specs=[ANY] * 6,
        out_specs=[VMEM] * 7,
        scratch_shapes=[
            pltpu.VMEM((QH, 1, tok), jnp.int32),
            pltpu.VMEM((1, tok), jnp.int32),
            pltpu.SemaphoreType.DMA((8,)),
        ],
        compiler_params=limit(6),
        name="split",
    )(*[in_hbm(value) for value in values])


def pack_kernel(tok, own, near, far, mine, send, sems):
    core = lax.rem(lax.axis_index("seq"), 2)
    rest = WINDOW - 2 * tok
    sides = ((mine, core), (send, 1 - core))
    pairs = []
    for target, side in sides:
        cols = pl.ds(pl.multiple_of(side * HD, HD), HD)
        pairs.append((own.at[:, cols], target.at[pl.ds(rest + tok, tok)]))
    copies = run_copies(pairs, sems)
    for target, side in sides:
        cols = pl.ds(pl.multiple_of(side * HD, HD), HD)
        target[:rest, :] = far[:, cols]
        target[rest : rest + tok, :] = near[:, cols]
    for copy in copies:
        copy.wait()


def pack(tok, own, near, far):
    half = jax.ShapeDtypeStruct((WINDOW, HD), bf16)
    return pl.pallas_call(
        functools.partial(pack_kernel, tok),
        out_shape=[half] * 2,
        in_specs=[ANY] + [VMEM] * 2,
        out_specs=[VMEM] * 2,
        scratch_shapes=[pltpu.SemaphoreType.DMA((2,))],
        compiler_params=limit(4),
        name="pack",
    )(in_hbm(own), near, far)


def lay_out(core, tok, raw, q_buf, g_buf, k_buf):
    q_own, q_oth, g_own, g_oth, k_own, k_oth = raw
    rest = WINDOW - 2 * tok
    for own, oth, buf, first, begin in (
        (k_own, k_oth, k_buf, rest, rest),
        (k_own, k_oth, k_buf, rest + tok, WINDOW),
        (q_own, q_oth, q_buf, 0, 0),
        (g_own, g_oth, g_buf, 0, 0),
    ):
        buf[pl.ds(pl.multiple_of(begin + core * tok, 64), tok), :] = own[first : first + tok, :]
        buf[pl.ds(pl.multiple_of(begin + (1 - core) * tok, 64), tok), :] = oth[
            first : first + tok, :
        ]
    k_buf[:rest, :] = jnp.where(core == 1, k_own[:rest, :], k_oth[:rest, :])


def head_masks(core, own, oth):
    spikes = jnp.where(
        core == 0,
        jnp.concatenate([own, oth], axis=1),
        jnp.concatenate([oth, own], axis=1),
    ).astype(f32)
    return jnp.where(core == 0, spikes[:GROUP], spikes[GROUP:])


def biases(chip, tok, block):
    later = lax.broadcasted_iota(jnp.int32, (BLOCK, BLOCK), 0)
    query = lax.broadcasted_iota(jnp.int32, (BLOCK, BLOCK), 1)
    first_key = WINDOW - chip * 2 * tok
    tiles = SPAN // BLOCK
    result = []
    for tile in range(tiles):
        begin = (block + tile) * BLOCK
        bias = None
        if begin < WINDOW:
            bias = jnp.where(begin >= first_key, 0.0, masked_score).astype(f32)
        if tile == 0:
            bias = jnp.where(later > query, bias if bias is not None else 0.0, masked_score)
        elif tile == tiles - 1:
            bias = jnp.where(later <= query, 0.0, masked_score)
        result.append(bias)
    return result


def dot_nt(a, b):
    return lax.dot_general(a, b, (((1,), (1,)), ((), ())), preferred_element_type=f32)


def dot_tn(a, b):
    return lax.dot_general(a, b, (((0,), (0,)), ((), ())), preferred_element_type=f32)


def masked(scores, bias):
    tiles = [scores[n * BLOCK : (n + 1) * BLOCK] for n in range(len(bias))]
    return jnp.concatenate(
        [tile if add is None else tile + add for tile, add in zip(tiles, bias)], axis=0
    )


def stacked(buf, block):
    rows = slice(block * BLOCK, (block + 1) * BLOCK)
    return jnp.concatenate(
        [buf[rows, head * HD : (head + 1) * HD] for head in range(GROUP)], axis=0
    )


def value_kernel(tok, *refs):
    raw, m_own, m_oth = refs[:6], *refs[6:8]
    own_out, near_out, far_out, top_out, norm_out = refs[8:13]
    q_buf, g_buf, k_buf, p_buf, acc = refs[13:]
    place = lax.axis_index("seq")
    core, chip = lax.rem(place, 2), lax.div(place, 2)
    lay_out(core, tok, raw, q_buf, g_buf, k_buf)
    spikes = head_masks(core, m_own[:QH, :], m_oth[:QH, :])
    acc[...] = jnp.zeros_like(acc)
    for block in range(2 * tok // BLOCK):
        bias = biases(chip, tok, block)
        begin = block * BLOCK
        rows = slice(begin, begin + BLOCK)
        keys = k_buf[begin : begin + SPAN, :]
        for head in range(GROUP):
            cols = slice(head * HD, (head + 1) * HD)
            scores = masked(dot_nt(keys, q_buf[rows, cols]), bias)
            top = jnp.max(scores, axis=0, keepdims=True)
            expo = jnp.exp2((scores - top) * exp2_scale)
            norm = spikes[head : head + 1, rows] / jnp.sum(expo, axis=0, keepdims=True)
            p_buf[:, cols] = (expo * norm).astype(bf16)
            at = block * GROUP + head
            top_out[at : at + 1, :] = top
            norm_out[at : at + 1, :] = norm
        acc[begin : begin + SPAN, :] += jnp.dot(
            p_buf[...], stacked(g_buf, block), preferred_element_type=f32
        )
    rest = WINDOW - 2 * tok
    far_out[...] = acc[:rest, :].astype(bf16)
    near_out[...] = acc[rest:WINDOW, :].astype(bf16)
    own_out[...] = acc[WINDOW:, :]


def key_kernel(tok, *refs):
    raw = refs[:6]
    top_in, norm_in, v_own, v_near, v_far = refs[6:11]
    own_out, near_out, far_out, mine_out, send_out = refs[11:16]
    q_buf, g_buf, k_buf, v_buf, d_buf, acc, r_buf = refs[16:]
    place = lax.axis_index("seq")
    core, chip = lax.rem(place, 2), lax.div(place, 2)
    rest = WINDOW - 2 * tok
    lay_out(core, tok, raw, q_buf, g_buf, k_buf)
    v_buf[:rest, :] = v_far[...]
    v_buf[rest:WINDOW, :] = v_near[...]
    v_buf[WINDOW:, :] = v_own[...]
    acc[...] = jnp.zeros_like(acc)
    for block in range(2 * tok // BLOCK):
        bias = biases(chip, tok, block)
        begin = block * BLOCK
        rows = slice(begin, begin + BLOCK)
        keys = k_buf[begin : begin + SPAN, :]
        values = v_buf[begin : begin + SPAN, :]
        for head in range(GROUP):
            cols = slice(head * HD, (head + 1) * HD)
            at = block * GROUP + head
            scores = masked(dot_nt(keys, q_buf[rows, cols]), bias)
            probs = jnp.exp2((scores - top_in[at : at + 1, :]) * exp2_scale)
            probs = probs * norm_in[at : at + 1, :]
            prob_grad = dot_nt(values, g_buf[rows, cols])
            delta = jnp.sum(probs.astype(bf16).astype(f32) * prob_grad, axis=0, keepdims=True)
            d_buf[:, cols] = (probs * (prob_grad - delta)).astype(bf16)
        acc[begin : begin + SPAN, :] += jnp.dot(
            d_buf[...], stacked(q_buf, block), preferred_element_type=f32
        )
        query_part = dot_tn(d_buf[...], keys) * score_scale
        for head in range(GROUP):
            cols = slice(head * HD, (head + 1) * HD)
            r_buf[rows, cols] = query_part[head * BLOCK : (head + 1) * BLOCK].astype(bf16)
    mine_out[...] = r_buf[pl.ds(pl.multiple_of(core * tok, 64), tok), :]
    send_out[...] = r_buf[pl.ds(pl.multiple_of((1 - core) * tok, 64), tok), :]
    far_out[...] = (acc[:rest, :] * score_scale).astype(bf16)
    near_out[...] = (acc[rest:WINDOW, :] * score_scale).astype(bf16)
    own_out[...] = acc[WINDOW:, :] * score_scale


def head_scratch(tok):
    return [
        pltpu.VMEM((2 * tok, GROUP * HD), bf16),
        pltpu.VMEM((2 * tok, GROUP * HD), bf16),
        pltpu.VMEM((WINDOW + 2 * tok, HD), bf16),
    ]


def term_shapes(tok):
    return [
        jax.ShapeDtypeStruct((2 * tok, HD), f32),
        jax.ShapeDtypeStruct((2 * tok, HD), bf16),
        jax.ShapeDtypeStruct((WINDOW - 2 * tok, HD), bf16),
    ]


def value_terms(tok, raw, spikes):
    stats = jax.ShapeDtypeStruct((2 * tok // BLOCK * GROUP, BLOCK), f32)
    return pl.pallas_call(
        functools.partial(value_kernel, tok),
        out_shape=term_shapes(tok) + [stats, stats],
        in_specs=[VMEM] * 8,
        out_specs=[VMEM] * 5,
        scratch_shapes=head_scratch(tok)
        + [
            pltpu.VMEM((SPAN, GROUP * HD), bf16),
            pltpu.VMEM((WINDOW + 2 * tok, HD), f32),
        ],
        compiler_params=limit(12),
        name="value_terms",
    )(*raw, *spikes)


def key_terms(tok, raw, top, norm, values):
    half = jax.ShapeDtypeStruct((tok, GROUP * HD), bf16)
    return pl.pallas_call(
        functools.partial(key_kernel, tok),
        out_shape=term_shapes(tok) + [half, half],
        in_specs=[VMEM] * 11,
        out_specs=[VMEM] * 5,
        scratch_shapes=head_scratch(tok)
        + [
            pltpu.VMEM((WINDOW + 2 * tok, HD), bf16),
            pltpu.VMEM((SPAN, GROUP * HD), bf16),
            pltpu.VMEM((WINDOW + 2 * tok, HD), f32),
            pltpu.VMEM((2 * tok, GROUP * HD), bf16),
        ],
        compiler_params=limit(14),
        name="key_terms",
    )(*raw, top, norm, *values)


def sum_keys_kernel(tok, own, near, far, mine, send, buf):
    core = lax.rem(lax.axis_index("seq"), 2)
    buf[...] = value_sum(tok, own[...], near[...], far[...])
    mine[...] = buf[pl.ds(pl.multiple_of(core * tok, 64), tok), :].astype(bf16)
    send[...] = buf[pl.ds(pl.multiple_of((1 - core) * tok, 64), tok), :].astype(bf16)


def sum_keys(tok, own, near, far):
    half = jax.ShapeDtypeStruct((tok, HD), bf16)
    return pl.pallas_call(
        functools.partial(sum_keys_kernel, tok),
        out_shape=[half, half],
        in_specs=[VMEM] * 3,
        out_specs=[VMEM] * 2,
        scratch_shapes=[pltpu.VMEM((2 * tok, HD), f32)],
        compiler_params=limit(4),
        name="sum_keys",
    )(own, near, far)


def column(row):
    size = row.shape[1]
    diagonal = lax.broadcasted_iota(jnp.int32, (size, size), 0) == lax.broadcasted_iota(
        jnp.int32, (size, size), 1
    )
    return jnp.sum(jnp.where(diagonal, row, 0.0), axis=1, keepdims=True)


def project_kernel(tok, split, h_own, h_oth, l_own, l_oth, w_own, w_oth, out, tail, spiked, w_buf, sems):
    core = lax.rem(lax.axis_index("seq"), 2)
    if split:
        row = lax.axis_index("dp")
        depth = w_own.shape[0]
        pairs = [
            (w_own, w_buf.at[pl.ds(pl.multiple_of(row * depth, depth), depth)]),
            (w_oth, w_buf.at[pl.ds(pl.multiple_of((1 - row) * depth, depth), depth)]),
        ]
    else:
        pairs = [(w_own, w_buf)]
    copies = run_copies(pairs, sems)
    for source, level, place in ((h_own, l_own, core), (h_oth, l_oth, 1 - core)):
        factor = column(level[QH : QH + 1, :].astype(f32) / LEVELS)
        rows = pl.ds(pl.multiple_of(place * tok, 64), tok)
        spiked[rows, :] = (source[...].astype(f32) * factor).astype(bf16)
    for copy in copies:
        copy.wait()
    values = jnp.dot(spiked[...], w_buf[...], preferred_element_type=f32).astype(bf16)
    out[...] = values
    tail[...] = values[4 * tok - WINDOW :, :]


def project(tok, hidden, levels, weight):
    depth = hidden[0].shape[1]
    split = len(weight) == 2
    return pl.pallas_call(
        functools.partial(project_kernel, tok, split),
        out_shape=[
            jax.ShapeDtypeStruct((2 * tok, HD), bf16),
            jax.ShapeDtypeStruct((WINDOW - 2 * tok, HD), bf16),
            jax.ShapeDtypeStruct((2 * tok, depth), bf16),
        ],
        in_specs=[VMEM] * 4 + [ANY] * 2,
        out_specs=[VMEM] * 3,
        scratch_shapes=[pltpu.VMEM((depth, HD), bf16), pltpu.SemaphoreType.DMA((2,))],
        compiler_params=limit(14),
        name="project",
    )(*hidden, *levels, weight[0], weight[-1])


def value_sum(tok, own, near, far):
    late = own[4 * tok - WINDOW :] + far.astype(f32)
    early = own[: 4 * tok - WINDOW]
    return jnp.concatenate([early, late], axis=0) + near.astype(f32)


def weight_kernel(tok, spiked, own, near, far, keep, send, w_buf):
    rows = spiked.shape[1] // 16
    value_grad = value_sum(tok, own[...], near[...], far[...]).astype(bf16)
    mine = block_code()
    for part in range(4):
        term = dot_tn(spiked[:, part * 4 * rows : (part + 1) * 4 * rows], value_grad)
        for piece in range(4):
            at = (part * 4 + piece) ^ mine
            w_buf[pl.ds(pl.multiple_of(at * rows, 16), rows), :] = term[
                piece * rows : (piece + 1) * rows
            ]
    keep[...] = w_buf[: 8 * rows, :]
    send[...] = w_buf[8 * rows :, :].astype(bf16)


def chip_bits():
    chip = lax.div(lax.axis_index("seq"), 2)
    return chip & 1, (chip >> 1) & 1, (chip >> 2) & 1


def block_code():
    return lax.axis_index("dp") * 8 + chip_code()


def chip_code():
    y, near, far = chip_bits()
    return y * 4 + near * 2 + far


def weight_terms(tok, spiked, terms):
    depth = spiked.shape[1]
    return pl.pallas_call(
        functools.partial(weight_kernel, tok),
        out_shape=[
            jax.ShapeDtypeStruct((depth // 2, HD), f32),
            jax.ShapeDtypeStruct((depth // 2, HD), bf16),
        ],
        in_specs=[VMEM] * 4,
        out_specs=[VMEM] * 2,
        scratch_shapes=[pltpu.VMEM((depth, HD), f32)],
        compiler_params=limit(14),
        name="weight_terms",
    )(spiked, *terms)


def reduce_kernel(count, turned, held, *refs):
    total = held[...].astype(f32)
    for got in refs[:count]:
        term = got[...].astype(f32)
        if turned:
            half = term.shape[0] // 2
            term = jnp.concatenate([term[half:], term[:half]], axis=0)
        total = total + term
    outs = refs[count:]
    rows = total.shape[0] // len(outs)
    outs[0][...] = total[:rows].astype(outs[0].dtype)
    for part in range(1, len(outs)):
        outs[part][...] = total[part * rows : (part + 1) * rows].astype(bf16)


def reduce_step(held, got, parts, turned=False):
    rows = held.shape[0] // parts
    shapes = [jax.ShapeDtypeStruct((rows, HD), bf16)] * parts
    if parts > 1:
        shapes[0] = jax.ShapeDtypeStruct((rows, HD), f32)
    return pl.pallas_call(
        functools.partial(reduce_kernel, len(got), turned),
        out_shape=shapes,
        in_specs=[VMEM] * (1 + len(got)),
        out_specs=[VMEM] * parts,
        compiler_params=limit(6),
        name="reduce_step",
    )(held, *got)


def place_weight_kernel(*refs):
    out, sems = refs[8:]
    core = lax.rem(lax.axis_index("seq"), 2)
    code = chip_code()
    rows = refs[0].shape[0] // 2
    pairs = []
    for pieces, side in ((refs[:4], core), (refs[4:8], 1 - core)):
        cols = pl.ds(pl.multiple_of(side * HD, HD), HD)
        for index in range(8):
            source = pieces[index // 2].at[pl.ds(index % 2 * rows, rows)]
            at = pl.ds(pl.multiple_of((index ^ code) * rows, 16), rows)
            pairs.append((source, out.at[at, cols]))
    for copy in run_copies(pairs, sems):
        copy.wait()


def place_weight(*pieces):
    return pl.pallas_call(
        place_weight_kernel,
        out_shape=jax.ShapeDtypeStruct((4 * pieces[0].shape[0], KVH * HD), bf16),
        in_specs=[ANY] * 8,
        out_specs=ANY,
        scratch_shapes=[pltpu.SemaphoreType.DMA((16,))],
        compiler_params=limit(2),
        name="place_weight",
    )(*pieces)


def place_tokens_kernel(q_own, q_oth, k_own, k_oth, q_out, k_out, sems):
    core = lax.rem(lax.axis_index("seq"), 2)
    pairs = []
    for own, oth, out in ((q_own, q_oth, q_out), (k_own, k_oth, k_out)):
        width = own.shape[1]
        for source, side in ((own, core), (oth, 1 - core)):
            cols = pl.ds(pl.multiple_of(side * width, HD), width)
            pairs.append((source, out.at[:, cols]))
    for copy in run_copies(pairs, sems):
        copy.wait()


def place_tokens(q_own, q_oth, k_own, k_oth):
    return pl.pallas_call(
        place_tokens_kernel,
        out_shape=[
            jax.ShapeDtypeStruct((own.shape[0], 2 * own.shape[1]), bf16) for own in (q_own, k_own)
        ],
        in_specs=[ANY] * 4,
        out_specs=[ANY] * 2,
        scratch_shapes=[pltpu.SemaphoreType.DMA((4,))],
        compiler_params=limit(2),
        name="place_tokens",
    )(q_own, q_oth, k_own, k_oth)


def reduce_any(spiked, value_grad):
    n_dp, n_seq = lax.axis_size("dp"), lax.axis_size("seq")
    place, row = lax.axis_index("seq"), lax.axis_index("dp")
    core, chip = place % 2, place // 2
    part = lax.dot_general(
        spiked, value_grad, (((0,), (0,)), ((), ())), preferred_element_type=f32
    )
    steps = [("dp", 1 << b, (row >> b) & 1) for b in range(n_dp.bit_length() - 2, -1, -1)]
    chip_steps = [
        ("seq", 2 << b, (chip >> b) & 1) for b in range((n_seq // 2).bit_length() - 1)
    ]
    for axis, flip, bit in steps + chip_steps:
        half = part.shape[0] // 2
        send = lax.dynamic_slice_in_dim(part, (1 - bit) * half, half, 0).astype(bf16)
        keep = lax.dynamic_slice_in_dim(part, bit * half, half, 0)
        part = keep + swapped(send, axis, flip).astype(f32)
    owned = part.astype(bf16)
    for axis, flip, bit in chip_steps[::-1]:
        owned = ordered(bit, owned, swapped(owned, axis, flip))
    return ordered(core, owned, swapped(owned, "seq", 1), axis=1)


def body(hidden_in, spike_level, value_weight, queries, key_states, spike_mask, out_grad):
    tok = hidden_in.shape[1]
    n_dp, n_seq = lax.axis_size("dp"), lax.axis_size("seq")
    assert 0 < WINDOW - 2 * tok <= tok and 2 * tok % BLOCK == 0

    def both(value):
        return value, swapped(value, "seq", 1)

    own_keys = key_states[0]
    query_own, query_out, grad_own, grad_out, marks_own, weight_half, key_tail = split(
        tok,
        queries[0],
        out_grad[0],
        jnp.transpose(spike_mask, (2, 0, 1)),
        spike_level,
        value_weight,
        own_keys,
    )
    near_keys, far_keys = lax.optimization_barrier(
        (shifted(own_keys, 2), shifted(key_tail, 4, cores=(1,)))
    )
    query_oth, grad_oth, marks_oth = (
        swapped(value, "seq", 1) for value in (query_out, grad_out, marks_own)
    )
    near_keys, far_keys, query_oth, grad_oth, marks_oth = lax.optimization_barrier(
        (near_keys, far_keys, query_oth, grad_oth, marks_oth)
    )
    keys_own, keys_out = pack(tok, own_keys, near_keys, far_keys)
    if n_dp == 2:
        weight = (weight_half, swapped(weight_half, "dp", 1))
    else:
        weight = (lax.all_gather(weight_half, "dp", axis=0, tiled=True),)
    keys_oth, hidden_own, *weight = lax.optimization_barrier(
        (swapped(keys_out, "seq", 1), hidden_in[0], *weight)
    )
    raw = [query_own, query_oth, grad_own, grad_oth, keys_own, keys_oth]
    marks = (marks_own, marks_oth)

    own, near, far, top, norm = value_terms(tok, raw, marks)
    near, far = shifted(near, -2), shifted(far, -4)
    values, tail, spiked = project(tok, both(hidden_own), marks, weight)

    fast = n_dp == 2 and n_seq == 16 and hidden_in.shape[2] % 256 == 0
    if fast:
        keep, send = weight_terms(tok, spiked, (own, near, far))
        values, tail, send = lax.optimization_barrier((values, tail, send))
        got = crossed(send, n_seq)
    window = (values, shifted(values, 2), shifted(tail, 4))
    own_k, near_k, far_k, query_mine, query_out = key_terms(tok, raw, top, norm, window)
    if fast:
        got, own_k = lax.optimization_barrier((got, own_k))
        keep, *sends = reduce_step(keep, [got], 4)
        near_k, far_k, *sends = lax.optimization_barrier((near_k, far_k, *sends))
        got = [crossed(send, flip) for send, flip in zip(sends, (4, 2, 6))]
    near_k, far_k = shifted(near_k, -2), shifted(far_k, -4)
    if fast:
        (part,) = reduce_step(keep, got, 1)
        query_out, part = lax.optimization_barrier((query_out, part))
        got = crossed(part, 8)
    query_got = swapped(query_out, "seq", 1)
    if fast:
        got, near_k, far_k, query_got = lax.optimization_barrier((got, near_k, far_k, query_got))
        (owned,) = reduce_step(part, [got], 1, turned=True)
        near_k, owned = lax.optimization_barrier((near_k, owned))
    key_mine, key_out = sum_keys(tok, own_k, near_k, far_k)
    key_got = swapped(key_out, "seq", 1)
    query_grad, key_grad = place_tokens(query_mine, query_got, key_mine, key_got)
    if fast:
        pieces = [crossed(owned, flip) for flip in (4, 2, 6)]
        *pieces, key_grad = lax.optimization_barrier((*pieces, key_grad))
        pieces = [owned, *pieces]
        weight_grad = place_weight(*pieces, *[swapped(piece, "seq", 1) for piece in pieces])
    else:
        value_grad = value_sum(tok, own, near, far).astype(bf16)
        weight_grad = reduce_any(spiked, value_grad)
    return (query_grad[None], key_grad[None], weight_grad)


def solution(mesh):
    placed = (
        P("dp", "seq", None),
        P("dp", "seq"),
        P("dp", None),
        P("dp", "seq", None),
        P("dp", "seq", None),
        P("dp", "seq", None),
        P("dp", "seq", None),
    )
    return jax.shard_map(
        body,
        mesh=mesh,
        in_specs=placed,
        out_specs=(P("dp", "seq", None), P("dp", "seq", None), P("dp", None)),
        check_vma=False,
    )
```

```python
import functools
import math

import jax
import jax.numpy as jnp
from jax import lax
from jax.experimental import pallas as pl
from jax.experimental.pallas import tpu as pltpu
from jax.sharding import PartitionSpec as P

QH = 14
KVH = 2
HD = 128
WINDOW = 512
LEVELS = 4
GROUP = 7
BLOCK = 128
SPAN = WINDOW + BLOCK

masked_score = -1e30
score_scale = 1.0 / math.sqrt(HD)
exp2_scale = score_scale * math.log2(math.e)

bf16 = jnp.bfloat16
f32 = jnp.float32
ANY = pl.BlockSpec(memory_space=pltpu.HBM)
VMEM = pl.BlockSpec(memory_space=pltpu.VMEM)


def limit(mib):
    return pltpu.CompilerParams(vmem_limit_bytes=mib * 1024 * 1024)


def shifted(value, steps, cores=(0, 1)):
    count = lax.axis_size("seq")
    pairs = [(i, (i + steps) % count) for i in range(count) if i % 2 in cores]
    return lax.ppermute(value, "seq", pairs)


def swapped(value, axis, flip):
    return lax.ppermute(value, axis, [(i, i ^ flip) for i in range(lax.axis_size(axis))])


def crossed(value, flip):
    count = lax.axis_size("dp") * lax.axis_size("seq")
    return lax.ppermute(value, ("dp", "seq"), [(i, i ^ flip) for i in range(count)])


def ordered(bit, own, other, axis=0):
    return jnp.where(
        bit == 0,
        jnp.concatenate([own, other], axis=axis),
        jnp.concatenate([other, own], axis=axis),
    )


def run_copies(pairs, sems):
    copies = [pltpu.make_async_copy(src, dst, sems.at[n]) for n, (src, dst) in enumerate(pairs)]
    for copy in copies:
        copy.start()
    return copies


def split_kernel(
    tok, q_ref, g_ref, m_ref, l_ref, w_ref, k_ref, *rest
):
    q_own, q_send, g_own, g_send, marks, w_half, k_tail, m_buf, l_buf, sems = rest
    core = lax.rem(lax.axis_index("seq"), 2)
    wide = GROUP * HD
    slim = pl.ds(pl.multiple_of(core * HD, HD), HD)
    pairs = [(m_ref, m_buf), (l_ref, l_buf), (w_ref.at[:, slim], w_half)]
    tail = k_tail.shape[0]
    pairs.append((k_ref.at[pl.ds(tok - tail, tail)], k_tail))
    for source, own, send in ((q_ref, q_own, q_send), (g_ref, g_own, g_send)):
        for target, side in ((own, core), (send, 1 - core)):
            pairs.append((source.at[:, pl.ds(pl.multiple_of(side * wide, HD), wide)], target))
    copies = run_copies(pairs, sems)
    for copy in copies:
        copy.wait()
    for head in range(QH):
        marks[head : head + 1, :] = m_buf[head]
    marks[QH : QH + 1, :] = l_buf[...]


def in_hbm(value):
    return pltpu.with_memory_space_constraint(value, pltpu.HBM)


def split(tok, *values):
    weight_rows = values[4].shape[0]
    half = jax.ShapeDtypeStruct((tok, GROUP * HD), bf16)
    return pl.pallas_call(
        functools.partial(split_kernel, tok),
        out_shape=[half] * 4
        + [
            jax.ShapeDtypeStruct((QH + 1, tok), jnp.int32),
            jax.ShapeDtypeStruct((weight_rows, HD), bf16),
            jax.ShapeDtypeStruct((WINDOW - 2 * tok, KVH * HD), bf16),
        ],
        in_specs=[ANY] * 6,
        out_specs=[VMEM] * 7,
        scratch_shapes=[
            pltpu.VMEM((QH, 1, tok), jnp.int32),
            pltpu.VMEM((1, tok), jnp.int32),
            pltpu.SemaphoreType.DMA((8,)),
        ],
        compiler_params=limit(6),
        name="split",
    )(*[in_hbm(value) for value in values])


def pack_kernel(tok, own, near, far, mine, send, sems):
    core = lax.rem(lax.axis_index("seq"), 2)
    rest = WINDOW - 2 * tok
    sides = ((mine, core), (send, 1 - core))
    pairs = []
    for target, side in sides:
        cols = pl.ds(pl.multiple_of(side * HD, HD), HD)
        pairs.append((own.at[:, cols], target.at[pl.ds(rest + tok, tok)]))
    copies = run_copies(pairs, sems)
    for target, side in sides:
        cols = pl.ds(pl.multiple_of(side * HD, HD), HD)
        target[:rest, :] = far[:, cols]
        target[rest : rest + tok, :] = near[:, cols]
    for copy in copies:
        copy.wait()


def pack(tok, own, near, far):
    half = jax.ShapeDtypeStruct((WINDOW, HD), bf16)
    return pl.pallas_call(
        functools.partial(pack_kernel, tok),
        out_shape=[half] * 2,
        in_specs=[ANY] + [VMEM] * 2,
        out_specs=[VMEM] * 2,
        scratch_shapes=[pltpu.SemaphoreType.DMA((2,))],
        compiler_params=limit(4),
        name="pack",
    )(in_hbm(own), near, far)


def lay_out(core, tok, raw, q_buf, g_buf, k_buf):
    q_own, q_oth, g_own, g_oth, k_own, k_oth = raw
    rest = WINDOW - 2 * tok
    for own, oth, buf, first, begin in (
        (k_own, k_oth, k_buf, rest, rest),
        (k_own, k_oth, k_buf, rest + tok, WINDOW),
        (q_own, q_oth, q_buf, 0, 0),
        (g_own, g_oth, g_buf, 0, 0),
    ):
        buf[pl.ds(pl.multiple_of(begin + core * tok, 64), tok), :] = own[first : first + tok, :]
        buf[pl.ds(pl.multiple_of(begin + (1 - core) * tok, 64), tok), :] = oth[
            first : first + tok, :
        ]
    k_buf[:rest, :] = jnp.where(core == 1, k_own[:rest, :], k_oth[:rest, :])


def head_masks(core, own, oth):
    spikes = jnp.where(
        core == 0,
        jnp.concatenate([own, oth], axis=1),
        jnp.concatenate([oth, own], axis=1),
    ).astype(f32)
    return jnp.where(core == 0, spikes[:GROUP], spikes[GROUP:])


def biases(chip, tok, block):
    later = lax.broadcasted_iota(jnp.int32, (BLOCK, BLOCK), 0)
    query = lax.broadcasted_iota(jnp.int32, (BLOCK, BLOCK), 1)
    first_key = WINDOW - chip * 2 * tok
    tiles = SPAN // BLOCK
    result = []
    for tile in range(tiles):
        begin = (block + tile) * BLOCK
        bias = None
        if begin < WINDOW:
            bias = jnp.where(begin >= first_key, 0.0, masked_score).astype(f32)
        if tile == 0:
            bias = jnp.where(later > query, bias if bias is not None else 0.0, masked_score)
        elif tile == tiles - 1:
            bias = jnp.where(later <= query, 0.0, masked_score)
        result.append(bias)
    return result


def dot_nt(a, b):
    return lax.dot_general(a, b, (((1,), (1,)), ((), ())), preferred_element_type=f32)


def dot_tn(a, b):
    return lax.dot_general(a, b, (((0,), (0,)), ((), ())), preferred_element_type=f32)


def masked(scores, bias):
    tiles = [scores[n * BLOCK : (n + 1) * BLOCK] for n in range(len(bias))]
    return jnp.concatenate(
        [tile if add is None else tile + add for tile, add in zip(tiles, bias)], axis=0
    )


def stacked(buf, block):
    rows = slice(block * BLOCK, (block + 1) * BLOCK)
    return jnp.concatenate(
        [buf[rows, head * HD : (head + 1) * HD] for head in range(GROUP)], axis=0
    )


def value_kernel(tok, *refs):
    raw, m_own, m_oth = refs[:6], *refs[6:8]
    own_out, near_out, far_out, top_out, norm_out = refs[8:13]
    q_buf, g_buf, k_buf, p_buf, acc = refs[13:]
    place = lax.axis_index("seq")
    core, chip = lax.rem(place, 2), lax.div(place, 2)
    lay_out(core, tok, raw, q_buf, g_buf, k_buf)
    spikes = head_masks(core, m_own[:QH, :], m_oth[:QH, :])
    acc[...] = jnp.zeros_like(acc)
    for block in range(2 * tok // BLOCK):
        bias = biases(chip, tok, block)
        begin = block * BLOCK
        rows = slice(begin, begin + BLOCK)
        keys = k_buf[begin : begin + SPAN, :]
        for head in range(GROUP):
            cols = slice(head * HD, (head + 1) * HD)
            scores = masked(dot_nt(keys, q_buf[rows, cols]), bias)
            top = jnp.max(scores, axis=0, keepdims=True)
            expo = jnp.exp2((scores - top) * exp2_scale)
            norm = spikes[head : head + 1, rows] / jnp.sum(expo, axis=0, keepdims=True)
            p_buf[:, cols] = (expo * norm).astype(bf16)
            at = block * GROUP + head
            top_out[at : at + 1, :] = top
            norm_out[at : at + 1, :] = norm
        acc[begin : begin + SPAN, :] += jnp.dot(
            p_buf[...], stacked(g_buf, block), preferred_element_type=f32
        )
    rest = WINDOW - 2 * tok
    far_out[...] = acc[:rest, :].astype(bf16)
    near_out[...] = acc[rest:WINDOW, :].astype(bf16)
    own_out[...] = acc[WINDOW:, :]


def key_kernel(tok, *refs):
    q_buf, g_buf, k_buf, top_in, norm_in, v_own, v_near, v_far = refs[:8]
    own_out, near_out, far_out, mine_out, send_out = refs[8:13]
    v_buf, d_buf, acc, r_buf = refs[13:]
    place = lax.axis_index("seq")
    core, chip = lax.rem(place, 2), lax.div(place, 2)
    rest = WINDOW - 2 * tok
    v_buf[:rest, :] = v_far[...]
    v_buf[rest:WINDOW, :] = v_near[...]
    v_buf[WINDOW:, :] = v_own[...]
    acc[...] = jnp.zeros_like(acc)
    for block in range(2 * tok // BLOCK):
        bias = biases(chip, tok, block)
        begin = block * BLOCK
        rows = slice(begin, begin + BLOCK)
        keys = k_buf[begin : begin + SPAN, :]
        values = v_buf[begin : begin + SPAN, :]
        for head in range(GROUP):
            cols = slice(head * HD, (head + 1) * HD)
            at = block * GROUP + head
            scores = masked(dot_nt(keys, q_buf[rows, cols]), bias)
            probs = jnp.exp2((scores - top_in[at : at + 1, :]) * exp2_scale)
            probs = probs * norm_in[at : at + 1, :]
            prob_grad = dot_nt(values, g_buf[rows, cols])
            delta = jnp.sum(probs.astype(bf16).astype(f32) * prob_grad, axis=0, keepdims=True)
            d_buf[:, cols] = (probs * (prob_grad - delta)).astype(bf16)
        acc[begin : begin + SPAN, :] += jnp.dot(
            d_buf[...], stacked(q_buf, block), preferred_element_type=f32
        )
        query_part = dot_tn(d_buf[...], keys) * score_scale
        for head in range(GROUP):
            cols = slice(head * HD, (head + 1) * HD)
            r_buf[rows, cols] = query_part[head * BLOCK : (head + 1) * BLOCK].astype(bf16)
    mine_out[...] = r_buf[pl.ds(pl.multiple_of(core * tok, 64), tok), :]
    send_out[...] = r_buf[pl.ds(pl.multiple_of((1 - core) * tok, 64), tok), :]
    far_out[...] = (acc[:rest, :] * score_scale).astype(bf16)
    near_out[...] = (acc[rest:WINDOW, :] * score_scale).astype(bf16)
    own_out[...] = acc[WINDOW:, :] * score_scale


def head_shapes(tok):
    return [
        jax.ShapeDtypeStruct((2 * tok, GROUP * HD), bf16),
        jax.ShapeDtypeStruct((2 * tok, GROUP * HD), bf16),
        jax.ShapeDtypeStruct((WINDOW + 2 * tok, HD), bf16),
    ]


def term_shapes(tok):
    return [
        jax.ShapeDtypeStruct((2 * tok, HD), f32),
        jax.ShapeDtypeStruct((2 * tok, HD), bf16),
        jax.ShapeDtypeStruct((WINDOW - 2 * tok, HD), bf16),
    ]


def value_terms(tok, raw, spikes):
    stats = jax.ShapeDtypeStruct((2 * tok // BLOCK * GROUP, BLOCK), f32)
    return pl.pallas_call(
        functools.partial(value_kernel, tok),
        out_shape=term_shapes(tok) + [stats, stats] + head_shapes(tok),
        in_specs=[VMEM] * 8,
        out_specs=[VMEM] * 8,
        scratch_shapes=[
            pltpu.VMEM((SPAN, GROUP * HD), bf16),
            pltpu.VMEM((WINDOW + 2 * tok, HD), f32),
        ],
        compiler_params=limit(12),
        name="value_terms",
    )(*raw, *spikes)


def key_terms(tok, heads, top, norm, values):
    half = jax.ShapeDtypeStruct((tok, GROUP * HD), bf16)
    return pl.pallas_call(
        functools.partial(key_kernel, tok),
        out_shape=term_shapes(tok) + [half, half],
        in_specs=[VMEM] * 8,
        out_specs=[VMEM] * 5,
        scratch_shapes=[
            pltpu.VMEM((WINDOW + 2 * tok, HD), bf16),
            pltpu.VMEM((SPAN, GROUP * HD), bf16),
            pltpu.VMEM((WINDOW + 2 * tok, HD), f32),
            pltpu.VMEM((2 * tok, GROUP * HD), bf16),
        ],
        compiler_params=limit(14),
        name="key_terms",
    )(*heads, top, norm, *values)


def sum_keys_kernel(tok, own, near, far, mine, send, buf):
    core = lax.rem(lax.axis_index("seq"), 2)
    buf[...] = value_sum(tok, own[...], near[...], far[...])
    mine[...] = buf[pl.ds(pl.multiple_of(core * tok, 64), tok), :].astype(bf16)
    send[...] = buf[pl.ds(pl.multiple_of((1 - core) * tok, 64), tok), :].astype(bf16)


def sum_keys(tok, own, near, far):
    half = jax.ShapeDtypeStruct((tok, HD), bf16)
    return pl.pallas_call(
        functools.partial(sum_keys_kernel, tok),
        out_shape=[half, half],
        in_specs=[VMEM] * 3,
        out_specs=[VMEM] * 2,
        scratch_shapes=[pltpu.VMEM((2 * tok, HD), f32)],
        compiler_params=limit(4),
        name="sum_keys",
    )(own, near, far)


def column(row):
    size = row.shape[1]
    diagonal = lax.broadcasted_iota(jnp.int32, (size, size), 0) == lax.broadcasted_iota(
        jnp.int32, (size, size), 1
    )
    return jnp.sum(jnp.where(diagonal, row, 0.0), axis=1, keepdims=True)


def project_kernel(tok, split, h_own, h_oth, l_own, l_oth, w_own, w_oth, out, tail, spiked, w_buf, sems):
    core = lax.rem(lax.axis_index("seq"), 2)
    if split:
        row = lax.axis_index("dp")
        depth = w_own.shape[0]
        pairs = [
            (w_own, w_buf.at[pl.ds(pl.multiple_of(row * depth, depth), depth)]),
            (w_oth, w_buf.at[pl.ds(pl.multiple_of((1 - row) * depth, depth), depth)]),
        ]
    else:
        pairs = [(w_own, w_buf)]
    copies = run_copies(pairs, sems)
    for source, level, place in ((h_own, l_own, core), (h_oth, l_oth, 1 - core)):
        factor = column(level[QH : QH + 1, :].astype(f32) / LEVELS)
        rows = pl.ds(pl.multiple_of(place * tok, 64), tok)
        spiked[rows, :] = (source[...].astype(f32) * factor).astype(bf16)
    for copy in copies:
        copy.wait()
    values = jnp.dot(spiked[...], w_buf[...], preferred_element_type=f32).astype(bf16)
    out[...] = values
    tail[...] = values[4 * tok - WINDOW :, :]


def project(tok, hidden, levels, weight):
    depth = hidden[0].shape[1]
    split = len(weight) == 2
    return pl.pallas_call(
        functools.partial(project_kernel, tok, split),
        out_shape=[
            jax.ShapeDtypeStruct((2 * tok, HD), bf16),
            jax.ShapeDtypeStruct((WINDOW - 2 * tok, HD), bf16),
            jax.ShapeDtypeStruct((2 * tok, depth), bf16),
        ],
        in_specs=[VMEM] * 4 + [ANY] * 2,
        out_specs=[VMEM] * 3,
        scratch_shapes=[pltpu.VMEM((depth, HD), bf16), pltpu.SemaphoreType.DMA((2,))],
        compiler_params=limit(14),
        name="project",
    )(*hidden, *levels, weight[0], weight[-1])


def value_sum(tok, own, near, far):
    late = own[4 * tok - WINDOW :] + far.astype(f32)
    early = own[: 4 * tok - WINDOW]
    return jnp.concatenate([early, late], axis=0) + near.astype(f32)


def weight_kernel(tok, spiked, own, near, far, keep, send, w_buf):
    rows = spiked.shape[1] // 16
    value_grad = value_sum(tok, own[...], near[...], far[...]).astype(bf16)
    mine = block_code()
    for part in range(4):
        term = dot_tn(spiked[:, part * 4 * rows : (part + 1) * 4 * rows], value_grad)
        for piece in range(4):
            at = (part * 4 + piece) ^ mine
            w_buf[pl.ds(pl.multiple_of(at * rows, 16), rows), :] = term[
                piece * rows : (piece + 1) * rows
            ]
    keep[...] = w_buf[: 8 * rows, :]
    send[...] = w_buf[8 * rows :, :].astype(bf16)


def chip_bits():
    chip = lax.div(lax.axis_index("seq"), 2)
    return chip & 1, (chip >> 1) & 1, (chip >> 2) & 1


def block_code():
    return lax.axis_index("dp") * 8 + chip_code()


def chip_code():
    y, near, far = chip_bits()
    return y * 4 + near * 2 + far


def weight_terms(tok, spiked, terms):
    depth = spiked.shape[1]
    return pl.pallas_call(
        functools.partial(weight_kernel, tok),
        out_shape=[
            jax.ShapeDtypeStruct((depth // 2, HD), f32),
            jax.ShapeDtypeStruct((depth // 2, HD), bf16),
        ],
        in_specs=[VMEM] * 4,
        out_specs=[VMEM] * 2,
        scratch_shapes=[pltpu.VMEM((depth, HD), f32)],
        compiler_params=limit(14),
        name="weight_terms",
    )(spiked, *terms)


def reduce_kernel(count, turned, held, *refs):
    total = held[...].astype(f32)
    for got in refs[:count]:
        term = got[...].astype(f32)
        if turned:
            half = term.shape[0] // 2
            term = jnp.concatenate([term[half:], term[:half]], axis=0)
        total = total + term
    outs = refs[count:]
    rows = total.shape[0] // len(outs)
    outs[0][...] = total[:rows].astype(outs[0].dtype)
    for part in range(1, len(outs)):
        outs[part][...] = total[part * rows : (part + 1) * rows].astype(bf16)


def reduce_step(held, got, parts, turned=False):
    rows = held.shape[0] // parts
    shapes = [jax.ShapeDtypeStruct((rows, HD), bf16)] * parts
    if parts > 1:
        shapes[0] = jax.ShapeDtypeStruct((rows, HD), f32)
    return pl.pallas_call(
        functools.partial(reduce_kernel, len(got), turned),
        out_shape=shapes,
        in_specs=[VMEM] * (1 + len(got)),
        out_specs=[VMEM] * parts,
        compiler_params=limit(6),
        name="reduce_step",
    )(held, *got)


def place_weight_kernel(*refs):
    out, sems = refs[8:]
    core = lax.rem(lax.axis_index("seq"), 2)
    code = chip_code()
    rows = refs[0].shape[0] // 2
    pairs = []
    for pieces, side in ((refs[:4], core), (refs[4:8], 1 - core)):
        cols = pl.ds(pl.multiple_of(side * HD, HD), HD)
        for index in range(8):
            source = pieces[index // 2].at[pl.ds(index % 2 * rows, rows)]
            at = pl.ds(pl.multiple_of((index ^ code) * rows, 16), rows)
            pairs.append((source, out.at[at, cols]))
    for copy in run_copies(pairs, sems):
        copy.wait()


def place_weight(*pieces):
    return pl.pallas_call(
        place_weight_kernel,
        out_shape=jax.ShapeDtypeStruct((4 * pieces[0].shape[0], KVH * HD), bf16),
        in_specs=[ANY] * 8,
        out_specs=ANY,
        scratch_shapes=[pltpu.SemaphoreType.DMA((16,))],
        compiler_params=limit(2),
        name="place_weight",
    )(*pieces)


def place_tokens_kernel(q_own, q_oth, k_own, k_oth, q_out, k_out, sems):
    core = lax.rem(lax.axis_index("seq"), 2)
    pairs = []
    for own, oth, out in ((q_own, q_oth, q_out), (k_own, k_oth, k_out)):
        width = own.shape[1]
        for source, side in ((own, core), (oth, 1 - core)):
            cols = pl.ds(pl.multiple_of(side * width, HD), width)
            pairs.append((source, out.at[:, cols]))
    for copy in run_copies(pairs, sems):
        copy.wait()


def place_tokens(q_own, q_oth, k_own, k_oth):
    return pl.pallas_call(
        place_tokens_kernel,
        out_shape=[
            jax.ShapeDtypeStruct((own.shape[0], 2 * own.shape[1]), bf16) for own in (q_own, k_own)
        ],
        in_specs=[ANY] * 4,
        out_specs=[ANY] * 2,
        scratch_shapes=[pltpu.SemaphoreType.DMA((4,))],
        compiler_params=limit(2),
        name="place_tokens",
    )(q_own, q_oth, k_own, k_oth)


def reduce_any(spiked, value_grad):
    n_dp, n_seq = lax.axis_size("dp"), lax.axis_size("seq")
    place, row = lax.axis_index("seq"), lax.axis_index("dp")
    core, chip = place % 2, place // 2
    part = lax.dot_general(
        spiked, value_grad, (((0,), (0,)), ((), ())), preferred_element_type=f32
    )
    steps = [("dp", 1 << b, (row >> b) & 1) for b in range(n_dp.bit_length() - 2, -1, -1)]
    chip_steps = [
        ("seq", 2 << b, (chip >> b) & 1) for b in range((n_seq // 2).bit_length() - 1)
    ]
    for axis, flip, bit in steps + chip_steps:
        half = part.shape[0] // 2
        send = lax.dynamic_slice_in_dim(part, (1 - bit) * half, half, 0).astype(bf16)
        keep = lax.dynamic_slice_in_dim(part, bit * half, half, 0)
        part = keep + swapped(send, axis, flip).astype(f32)
    owned = part.astype(bf16)
    for axis, flip, bit in chip_steps[::-1]:
        owned = ordered(bit, owned, swapped(owned, axis, flip))
    return ordered(core, owned, swapped(owned, "seq", 1), axis=1)


def body(hidden_in, spike_level, value_weight, queries, key_states, spike_mask, out_grad):
    tok = hidden_in.shape[1]
    n_dp, n_seq = lax.axis_size("dp"), lax.axis_size("seq")
    assert 0 < WINDOW - 2 * tok <= tok and 2 * tok % BLOCK == 0

    def both(value):
        return value, swapped(value, "seq", 1)

    own_keys = key_states[0]
    query_own, query_out, grad_own, grad_out, marks_own, weight_half, key_tail = split(
        tok,
        queries[0],
        out_grad[0],
        jnp.transpose(spike_mask, (2, 0, 1)),
        spike_level,
        value_weight,
        own_keys,
    )
    near_keys, far_keys = lax.optimization_barrier(
        (shifted(own_keys, 2), shifted(key_tail, 4, cores=(1,)))
    )
    query_oth, grad_oth, marks_oth = (
        swapped(value, "seq", 1) for value in (query_out, grad_out, marks_own)
    )
    near_keys, far_keys, query_oth, grad_oth, marks_oth = lax.optimization_barrier(
        (near_keys, far_keys, query_oth, grad_oth, marks_oth)
    )
    keys_own, keys_out = pack(tok, own_keys, near_keys, far_keys)
    if n_dp == 2:
        weight = (weight_half, swapped(weight_half, "dp", 1))
    else:
        weight = (lax.all_gather(weight_half, "dp", axis=0, tiled=True),)
    keys_oth, hidden_own, *weight = lax.optimization_barrier(
        (swapped(keys_out, "seq", 1), hidden_in[0], *weight)
    )
    raw = [query_own, query_oth, grad_own, grad_oth, keys_own, keys_oth]
    marks = (marks_own, marks_oth)

    own, near, far, top, norm, *heads = value_terms(tok, raw, marks)
    near, far = shifted(near, -2), shifted(far, -4)
    values, tail, spiked = project(tok, both(hidden_own), marks, weight)

    fast = n_dp == 2 and n_seq == 16 and hidden_in.shape[2] % 256 == 0
    if fast:
        keep, send = weight_terms(tok, spiked, (own, near, far))
        values, tail, send = lax.optimization_barrier((values, tail, send))
        got = crossed(send, n_seq)
    window = (values, shifted(values, 2), shifted(tail, 4))
    own_k, near_k, far_k, query_mine, query_out = key_terms(tok, heads, top, norm, window)
    if fast:
        got, own_k = lax.optimization_barrier((got, own_k))
        keep, *sends = reduce_step(keep, [got], 4)
        near_k, far_k, *sends = lax.optimization_barrier((near_k, far_k, *sends))
        got = [crossed(send, flip) for send, flip in zip(sends, (4, 2, 6))]
    near_k, far_k = shifted(near_k, -2), shifted(far_k, -4)
    if fast:
        (part,) = reduce_step(keep, got, 1)
        query_out, part = lax.optimization_barrier((query_out, part))
        got = crossed(part, 8)
    query_got = swapped(query_out, "seq", 1)
    if fast:
        got, near_k, far_k, query_got = lax.optimization_barrier((got, near_k, far_k, query_got))
        (owned,) = reduce_step(part, [got], 1, turned=True)
        near_k, owned = lax.optimization_barrier((near_k, owned))
    key_mine, key_out = sum_keys(tok, own_k, near_k, far_k)
    key_got = swapped(key_out, "seq", 1)
    query_grad, key_grad = place_tokens(query_mine, query_got, key_mine, key_got)
    if fast:
        pieces = [crossed(owned, flip) for flip in (4, 2, 6)]
        *pieces, key_grad = lax.optimization_barrier((*pieces, key_grad))
        pieces = [owned, *pieces]
        weight_grad = place_weight(*pieces, *[swapped(piece, "seq", 1) for piece in pieces])
    else:
        value_grad = value_sum(tok, own, near, far).astype(bf16)
        weight_grad = reduce_any(spiked, value_grad)
    return (query_grad[None], key_grad[None], weight_grad)


def solution(mesh):
    placed = (
        P("dp", "seq", None),
        P("dp", "seq"),
        P("dp", None),
        P("dp", "seq", None),
        P("dp", "seq", None),
        P("dp", "seq", None),
        P("dp", "seq", None),
    )
    return jax.shard_map(
        body,
        mesh=mesh,
        in_specs=placed,
        out_specs=(P("dp", "seq", None), P("dp", "seq", None), P("dp", None)),
        check_vma=False,
    )
```

```python
import functools
import math

import jax
import jax.numpy as jnp
from jax import lax
from jax.experimental import pallas as pl
from jax.experimental.pallas import tpu as pltpu
from jax.sharding import PartitionSpec as P

QH = 14
KVH = 2
HD = 128
WINDOW = 512
LEVELS = 4
GROUP = 7
BLOCK = 128
SPAN = WINDOW + BLOCK

masked_score = -1e30
score_scale = 1.0 / math.sqrt(HD)
exp2_scale = score_scale * math.log2(math.e)

bf16 = jnp.bfloat16
f32 = jnp.float32
ANY = pl.BlockSpec(memory_space=pltpu.HBM)
VMEM = pl.BlockSpec(memory_space=pltpu.VMEM)


def limit(mib):
    return pltpu.CompilerParams(vmem_limit_bytes=mib * 1024 * 1024)


def shifted(value, steps):
    count = lax.axis_size("seq")
    return lax.ppermute(value, "seq", [(i, (i + steps) % count) for i in range(count)])


def shifted_odd(value, steps):
    count = lax.axis_size("seq")
    return lax.ppermute(value, "seq", [(i, i + steps) for i in range(1, count - steps, 2)])


def swapped(value, axis, flip):
    return lax.ppermute(value, axis, [(i, i ^ flip) for i in range(lax.axis_size(axis))])


def crossed(value, flip):
    count = lax.axis_size("dp") * lax.axis_size("seq")
    return lax.ppermute(value, ("dp", "seq"), [(i, i ^ flip) for i in range(count)])


def ordered(bit, own, other, axis=0):
    return jnp.where(
        bit == 0,
        jnp.concatenate([own, other], axis=axis),
        jnp.concatenate([other, own], axis=axis),
    )


def run_copies(pairs, sems):
    copies = [pltpu.make_async_copy(src, dst, sems.at[n]) for n, (src, dst) in enumerate(pairs)]
    for copy in copies:
        copy.start()
    return copies


def split_kernel(
    tok, q_ref, g_ref, m_ref, l_ref, w_ref, k_ref, *rest
):
    q_own, q_send, g_own, g_send, marks, w_half, k_tail, m_buf, l_buf, sems = rest
    core = lax.rem(lax.axis_index("seq"), 2)
    wide = GROUP * HD
    slim = pl.ds(pl.multiple_of(core * HD, HD), HD)
    pairs = [(m_ref, m_buf), (l_ref, l_buf), (w_ref.at[:, slim], w_half)]
    tail = k_tail.shape[0]
    pairs.append((k_ref.at[pl.ds(tok - tail, tail)], k_tail))
    for source, own, send in ((q_ref, q_own, q_send), (g_ref, g_own, g_send)):
        for target, side in ((own, core), (send, 1 - core)):
            pairs.append((source.at[:, pl.ds(pl.multiple_of(side * wide, HD), wide)], target))
    copies = run_copies(pairs, sems)
    for copy in copies:
        copy.wait()
    for head in range(QH):
        marks[head : head + 1, :] = m_buf[head]
    marks[QH : QH + 1, :] = l_buf[...]


def in_hbm(value):
    return pltpu.with_memory_space_constraint(value, pltpu.HBM)


def split(tok, *values):
    weight_rows = values[4].shape[0]
    half = jax.ShapeDtypeStruct((tok, GROUP * HD), bf16)
    return pl.pallas_call(
        functools.partial(split_kernel, tok),
        out_shape=[half] * 4
        + [
            jax.ShapeDtypeStruct((QH + 1, tok), jnp.int32),
            jax.ShapeDtypeStruct((weight_rows, HD), bf16),
            jax.ShapeDtypeStruct((WINDOW - 2 * tok, KVH * HD), bf16),
        ],
        in_specs=[ANY] * 6,
        out_specs=[VMEM] * 7,
        scratch_shapes=[
            pltpu.VMEM((QH, 1, tok), jnp.int32),
            pltpu.VMEM((1, tok), jnp.int32),
            pltpu.SemaphoreType.DMA((8,)),
        ],
        compiler_params=limit(6),
        name="split",
    )(*[in_hbm(value) for value in values])


def pack_kernel(tok, own, near, far, mine, send, sems):
    core = lax.rem(lax.axis_index("seq"), 2)
    rest = WINDOW - 2 * tok
    sides = ((mine, core), (send, 1 - core))
    pairs = []
    for target, side in sides:
        cols = pl.ds(pl.multiple_of(side * HD, HD), HD)
        pairs.append((own.at[:, cols], target.at[pl.ds(rest + tok, tok)]))
    copies = run_copies(pairs, sems)
    for target, side in sides:
        cols = pl.ds(pl.multiple_of(side * HD, HD), HD)
        target[:rest, :] = far[:, cols]
        target[rest : rest + tok, :] = near[:, cols]
    for copy in copies:
        copy.wait()


def pack(tok, own, near, far):
    half = jax.ShapeDtypeStruct((WINDOW, HD), bf16)
    return pl.pallas_call(
        functools.partial(pack_kernel, tok),
        out_shape=[half] * 2,
        in_specs=[ANY] + [VMEM] * 2,
        out_specs=[VMEM] * 2,
        scratch_shapes=[pltpu.SemaphoreType.DMA((2,))],
        compiler_params=limit(4),
        name="pack",
    )(in_hbm(own), near, far)


def lay_out(core, tok, raw, q_buf, g_buf, k_buf):
    q_own, q_oth, g_own, g_oth, k_own, k_oth = raw
    rest = WINDOW - 2 * tok
    for own, oth, buf, first, begin in (
        (k_own, k_oth, k_buf, rest, rest),
        (k_own, k_oth, k_buf, rest + tok, WINDOW),
        (q_own, q_oth, q_buf, 0, 0),
        (g_own, g_oth, g_buf, 0, 0),
    ):
        buf[pl.ds(pl.multiple_of(begin + core * tok, 64), tok), :] = own[first : first + tok, :]
        buf[pl.ds(pl.multiple_of(begin + (1 - core) * tok, 64), tok), :] = oth[
            first : first + tok, :
        ]
    k_buf[:rest, :] = jnp.where(core == 1, k_own[:rest, :], k_oth[:rest, :])


def head_masks(core, own, oth):
    spikes = jnp.where(
        core == 0,
        jnp.concatenate([own, oth], axis=1),
        jnp.concatenate([oth, own], axis=1),
    ).astype(f32)
    return jnp.where(core == 0, spikes[:GROUP], spikes[GROUP:])


def biases(chip, tok, block):
    later = lax.broadcasted_iota(jnp.int32, (BLOCK, BLOCK), 0)
    query = lax.broadcasted_iota(jnp.int32, (BLOCK, BLOCK), 1)
    first_key = WINDOW - chip * 2 * tok
    tiles = SPAN // BLOCK
    result = []
    for tile in range(tiles):
        begin = (block + tile) * BLOCK
        bias = None
        if begin < WINDOW:
            bias = jnp.where(begin >= first_key, 0.0, masked_score).astype(f32)
        if tile == 0:
            bias = jnp.where(later > query, bias if bias is not None else 0.0, masked_score)
        elif tile == tiles - 1:
            bias = jnp.where(later <= query, 0.0, masked_score)
        result.append(bias)
    return result


def dot_nt(a, b):
    return lax.dot_general(a, b, (((1,), (1,)), ((), ())), preferred_element_type=f32)


def dot_tn(a, b):
    return lax.dot_general(a, b, (((0,), (0,)), ((), ())), preferred_element_type=f32)


def masked(scores, bias):
    tiles = [scores[n * BLOCK : (n + 1) * BLOCK] for n in range(len(bias))]
    return jnp.concatenate(
        [tile if add is None else tile + add for tile, add in zip(tiles, bias)], axis=0
    )


def stacked(buf, block):
    rows = slice(block * BLOCK, (block + 1) * BLOCK)
    return jnp.concatenate(
        [buf[rows, head * HD : (head + 1) * HD] for head in range(GROUP)], axis=0
    )


def value_kernel(tok, *refs):
    raw, m_own, m_oth = refs[:6], *refs[6:8]
    own_out, near_out, far_out, top_out, norm_out = refs[8:13]
    q_buf, g_buf, k_buf, p_buf, acc = refs[13:]
    place = lax.axis_index("seq")
    core, chip = lax.rem(place, 2), lax.div(place, 2)
    lay_out(core, tok, raw, q_buf, g_buf, k_buf)
    spikes = head_masks(core, m_own[:QH, :], m_oth[:QH, :])
    acc[...] = jnp.zeros_like(acc)
    for block in range(2 * tok // BLOCK):
        bias = biases(chip, tok, block)
        begin = block * BLOCK
        rows = slice(begin, begin + BLOCK)
        keys = k_buf[begin : begin + SPAN, :]
        for head in range(GROUP):
            cols = slice(head * HD, (head + 1) * HD)
            scores = masked(dot_nt(keys, q_buf[rows, cols]), bias)
            top = jnp.max(scores, axis=0, keepdims=True)
            expo = jnp.exp2((scores - top) * exp2_scale)
            norm = spikes[head : head + 1, rows] / jnp.sum(expo, axis=0, keepdims=True)
            p_buf[:, cols] = (expo * norm).astype(bf16)
            at = block * GROUP + head
            top_out[at : at + 1, :] = top
            norm_out[at : at + 1, :] = norm
        acc[begin : begin + SPAN, :] += jnp.dot(
            p_buf[...], stacked(g_buf, block), preferred_element_type=f32
        )
    rest = WINDOW - 2 * tok
    far_out[...] = acc[:rest, :].astype(bf16)
    near_out[...] = acc[rest:WINDOW, :].astype(bf16)
    own_out[...] = acc[WINDOW:, :]


def key_kernel(tok, *refs):
    q_buf, g_buf, k_buf, top_in, norm_in, v_own, v_near, v_far = refs[:8]
    own_out, near_out, far_out, mine_out, send_out = refs[8:13]
    v_buf, d_buf, acc, r_buf = refs[13:]
    place = lax.axis_index("seq")
    core, chip = lax.rem(place, 2), lax.div(place, 2)
    rest = WINDOW - 2 * tok
    v_buf[:rest, :] = v_far[...]
    v_buf[rest:WINDOW, :] = v_near[...]
    v_buf[WINDOW:, :] = v_own[...]
    acc[...] = jnp.zeros_like(acc)
    for block in range(2 * tok // BLOCK):
        bias = biases(chip, tok, block)
        begin = block * BLOCK
        rows = slice(begin, begin + BLOCK)
        keys = k_buf[begin : begin + SPAN, :]
        values = v_buf[begin : begin + SPAN, :]
        for head in range(GROUP):
            cols = slice(head * HD, (head + 1) * HD)
            at = block * GROUP + head
            scores = masked(dot_nt(keys, q_buf[rows, cols]), bias)
            probs = jnp.exp2((scores - top_in[at : at + 1, :]) * exp2_scale)
            probs = probs * norm_in[at : at + 1, :]
            prob_grad = dot_nt(values, g_buf[rows, cols])
            delta = jnp.sum(probs.astype(bf16).astype(f32) * prob_grad, axis=0, keepdims=True)
            d_buf[:, cols] = (probs * (prob_grad - delta)).astype(bf16)
        acc[begin : begin + SPAN, :] += jnp.dot(
            d_buf[...], stacked(q_buf, block), preferred_element_type=f32
        )
        query_part = dot_tn(d_buf[...], keys) * score_scale
        for head in range(GROUP):
            cols = slice(head * HD, (head + 1) * HD)
            r_buf[rows, cols] = query_part[head * BLOCK : (head + 1) * BLOCK].astype(bf16)
    mine_out[...] = r_buf[pl.ds(pl.multiple_of(core * tok, 64), tok), :]
    send_out[...] = r_buf[pl.ds(pl.multiple_of((1 - core) * tok, 64), tok), :]
    far_out[...] = (acc[:rest, :] * score_scale).astype(bf16)
    near_out[...] = (acc[rest:WINDOW, :] * score_scale).astype(bf16)
    own_out[...] = acc[WINDOW:, :] * score_scale


def head_shapes(tok):
    return [
        jax.ShapeDtypeStruct((2 * tok, GROUP * HD), bf16),
        jax.ShapeDtypeStruct((2 * tok, GROUP * HD), bf16),
        jax.ShapeDtypeStruct((WINDOW + 2 * tok, HD), bf16),
    ]


def term_shapes(tok):
    return [
        jax.ShapeDtypeStruct((2 * tok, HD), f32),
        jax.ShapeDtypeStruct((2 * tok, HD), bf16),
        jax.ShapeDtypeStruct((WINDOW - 2 * tok, HD), bf16),
    ]


def value_terms(tok, raw, spikes):
    stats = jax.ShapeDtypeStruct((2 * tok // BLOCK * GROUP, BLOCK), f32)
    return pl.pallas_call(
        functools.partial(value_kernel, tok),
        out_shape=term_shapes(tok) + [stats, stats] + head_shapes(tok),
        in_specs=[VMEM] * 8,
        out_specs=[VMEM] * 8,
        scratch_shapes=[
            pltpu.VMEM((SPAN, GROUP * HD), bf16),
            pltpu.VMEM((WINDOW + 2 * tok, HD), f32),
        ],
        compiler_params=limit(12),
        name="value_terms",
    )(*raw, *spikes)


def key_terms(tok, heads, top, norm, values):
    half = jax.ShapeDtypeStruct((tok, GROUP * HD), bf16)
    return pl.pallas_call(
        functools.partial(key_kernel, tok),
        out_shape=term_shapes(tok) + [half, half],
        in_specs=[VMEM] * 8,
        out_specs=[VMEM] * 5,
        scratch_shapes=[
            pltpu.VMEM((WINDOW + 2 * tok, HD), bf16),
            pltpu.VMEM((SPAN, GROUP * HD), bf16),
            pltpu.VMEM((WINDOW + 2 * tok, HD), f32),
            pltpu.VMEM((2 * tok, GROUP * HD), bf16),
        ],
        compiler_params=limit(14),
        name="key_terms",
    )(*heads, top, norm, *values)


def sum_keys_kernel(tok, own, near, far, mine, send, buf):
    core = lax.rem(lax.axis_index("seq"), 2)
    buf[...] = value_sum(tok, own[...], near[...], far[...])
    mine[...] = buf[pl.ds(pl.multiple_of(core * tok, 64), tok), :].astype(bf16)
    send[...] = buf[pl.ds(pl.multiple_of((1 - core) * tok, 64), tok), :].astype(bf16)


def sum_keys(tok, own, near, far):
    half = jax.ShapeDtypeStruct((tok, HD), bf16)
    return pl.pallas_call(
        functools.partial(sum_keys_kernel, tok),
        out_shape=[half, half],
        in_specs=[VMEM] * 3,
        out_specs=[VMEM] * 2,
        scratch_shapes=[pltpu.VMEM((2 * tok, HD), f32)],
        compiler_params=limit(4),
        name="sum_keys",
    )(own, near, far)


def column(row):
    size = row.shape[1]
    diagonal = lax.broadcasted_iota(jnp.int32, (size, size), 0) == lax.broadcasted_iota(
        jnp.int32, (size, size), 1
    )
    return jnp.sum(jnp.where(diagonal, row, 0.0), axis=1, keepdims=True)


def project_kernel(tok, split, h_own, h_oth, l_own, l_oth, w_own, w_oth, out, tail, spiked, w_buf, sems):
    core = lax.rem(lax.axis_index("seq"), 2)
    if split:
        row = lax.axis_index("dp")
        depth = w_own.shape[0]
        pairs = [
            (w_own, w_buf.at[pl.ds(pl.multiple_of(row * depth, depth), depth)]),
            (w_oth, w_buf.at[pl.ds(pl.multiple_of((1 - row) * depth, depth), depth)]),
        ]
    else:
        pairs = [(w_own, w_buf)]
    copies = run_copies(pairs, sems)
    for source, level, place in ((h_own, l_own, core), (h_oth, l_oth, 1 - core)):
        factor = column(level[QH : QH + 1, :].astype(f32) / LEVELS)
        rows = pl.ds(pl.multiple_of(place * tok, 64), tok)
        spiked[rows, :] = (source[...].astype(f32) * factor).astype(bf16)
    for copy in copies:
        copy.wait()
    values = jnp.dot(spiked[...], w_buf[...], preferred_element_type=f32).astype(bf16)
    out[...] = values
    tail[...] = values[4 * tok - WINDOW :, :]


def project(tok, hidden, levels, weight):
    depth = hidden[0].shape[1]
    split = len(weight) == 2
    return pl.pallas_call(
        functools.partial(project_kernel, tok, split),
        out_shape=[
            jax.ShapeDtypeStruct((2 * tok, HD), bf16),
            jax.ShapeDtypeStruct((WINDOW - 2 * tok, HD), bf16),
            jax.ShapeDtypeStruct((2 * tok, depth), bf16),
        ],
        in_specs=[VMEM] * 4 + [ANY] * 2,
        out_specs=[VMEM] * 3,
        scratch_shapes=[pltpu.VMEM((depth, HD), bf16), pltpu.SemaphoreType.DMA((2,))],
        compiler_params=limit(14),
        name="project",
    )(*hidden, *levels, weight[0], weight[-1])


def value_sum(tok, own, near, far):
    late = own[4 * tok - WINDOW :] + far.astype(f32)
    early = own[: 4 * tok - WINDOW]
    return jnp.concatenate([early, late], axis=0) + near.astype(f32)


def weight_kernel(tok, spiked, own, near, far, keep, send, w_buf):
    rows = spiked.shape[1] // 16
    value_grad = value_sum(tok, own[...], near[...], far[...]).astype(bf16)
    mine = block_code()
    for part in range(4):
        term = dot_tn(spiked[:, part * 4 * rows : (part + 1) * 4 * rows], value_grad)
        for piece in range(4):
            at = (part * 4 + piece) ^ mine
            w_buf[pl.ds(pl.multiple_of(at * rows, 16), rows), :] = term[
                piece * rows : (piece + 1) * rows
            ]
    keep[...] = w_buf[: 8 * rows, :]
    send[...] = w_buf[8 * rows :, :].astype(bf16)


def chip_bits():
    chip = lax.div(lax.axis_index("seq"), 2)
    return chip & 1, (chip >> 1) & 1, (chip >> 2) & 1


def block_code():
    return lax.axis_index("dp") * 8 + chip_code()


def chip_code():
    y, near, far = chip_bits()
    return y * 4 + near * 2 + far


def weight_terms(tok, spiked, terms):
    depth = spiked.shape[1]
    return pl.pallas_call(
        functools.partial(weight_kernel, tok),
        out_shape=[
            jax.ShapeDtypeStruct((depth // 2, HD), f32),
            jax.ShapeDtypeStruct((depth // 2, HD), bf16),
        ],
        in_specs=[VMEM] * 4,
        out_specs=[VMEM] * 2,
        scratch_shapes=[pltpu.VMEM((depth, HD), f32)],
        compiler_params=limit(14),
        name="weight_terms",
    )(spiked, *terms)


def reduce_kernel(count, turned, held, *refs):
    total = held[...].astype(f32)
    for got in refs[:count]:
        term = got[...].astype(f32)
        if turned:
            half = term.shape[0] // 2
            term = jnp.concatenate([term[half:], term[:half]], axis=0)
        total = total + term
    outs = refs[count:]
    rows = total.shape[0] // len(outs)
    outs[0][...] = total[:rows].astype(outs[0].dtype)
    for part in range(1, len(outs)):
        outs[part][...] = total[part * rows : (part + 1) * rows].astype(bf16)


def reduce_step(held, got, parts, turned=False):
    rows = held.shape[0] // parts
    shapes = [jax.ShapeDtypeStruct((rows, HD), bf16)] * parts
    if parts > 1:
        shapes[0] = jax.ShapeDtypeStruct((rows, HD), f32)
    return pl.pallas_call(
        functools.partial(reduce_kernel, len(got), turned),
        out_shape=shapes,
        in_specs=[VMEM] * (1 + len(got)),
        out_specs=[VMEM] * parts,
        compiler_params=limit(6),
        name="reduce_step",
    )(held, *got)


def place_weight_kernel(*refs):
    out, sems = refs[8:]
    core = lax.rem(lax.axis_index("seq"), 2)
    code = chip_code()
    rows = refs[0].shape[0] // 2
    pairs = []
    for pieces, side in ((refs[:4], core), (refs[4:8], 1 - core)):
        cols = pl.ds(pl.multiple_of(side * HD, HD), HD)
        for index in range(8):
            source = pieces[index // 2].at[pl.ds(index % 2 * rows, rows)]
            at = pl.ds(pl.multiple_of((index ^ code) * rows, 16), rows)
            pairs.append((source, out.at[at, cols]))
    for copy in run_copies(pairs, sems):
        copy.wait()


def place_weight(*pieces):
    return pl.pallas_call(
        place_weight_kernel,
        out_shape=jax.ShapeDtypeStruct((4 * pieces[0].shape[0], KVH * HD), bf16),
        in_specs=[ANY] * 8,
        out_specs=ANY,
        scratch_shapes=[pltpu.SemaphoreType.DMA((16,))],
        compiler_params=limit(2),
        name="place_weight",
    )(*pieces)


def place_tokens_kernel(q_own, q_oth, k_own, k_oth, q_out, k_out, sems):
    core = lax.rem(lax.axis_index("seq"), 2)
    pairs = []
    for own, oth, out in ((q_own, q_oth, q_out), (k_own, k_oth, k_out)):
        width = own.shape[1]
        for source, side in ((own, core), (oth, 1 - core)):
            cols = pl.ds(pl.multiple_of(side * width, HD), width)
            pairs.append((source, out.at[:, cols]))
    for copy in run_copies(pairs, sems):
        copy.wait()


def place_tokens(q_own, q_oth, k_own, k_oth):
    return pl.pallas_call(
        place_tokens_kernel,
        out_shape=[
            jax.ShapeDtypeStruct((own.shape[0], 2 * own.shape[1]), bf16) for own in (q_own, k_own)
        ],
        in_specs=[ANY] * 4,
        out_specs=[ANY] * 2,
        scratch_shapes=[pltpu.SemaphoreType.DMA((4,))],
        compiler_params=limit(2),
        name="place_tokens",
    )(q_own, q_oth, k_own, k_oth)


def reduce_any(spiked, value_grad):
    n_dp, n_seq = lax.axis_size("dp"), lax.axis_size("seq")
    place, row = lax.axis_index("seq"), lax.axis_index("dp")
    core, chip = place % 2, place // 2
    part = lax.dot_general(
        spiked, value_grad, (((0,), (0,)), ((), ())), preferred_element_type=f32
    )
    steps = [("dp", 1 << b, (row >> b) & 1) for b in range(n_dp.bit_length() - 2, -1, -1)]
    chip_steps = [
        ("seq", 2 << b, (chip >> b) & 1) for b in range((n_seq // 2).bit_length() - 1)
    ]
    for axis, flip, bit in steps + chip_steps:
        half = part.shape[0] // 2
        send = lax.dynamic_slice_in_dim(part, (1 - bit) * half, half, 0).astype(bf16)
        keep = lax.dynamic_slice_in_dim(part, bit * half, half, 0)
        part = keep + swapped(send, axis, flip).astype(f32)
    owned = part.astype(bf16)
    for axis, flip, bit in chip_steps[::-1]:
        owned = ordered(bit, owned, swapped(owned, axis, flip))
    return ordered(core, owned, swapped(owned, "seq", 1), axis=1)


def body(hidden_in, spike_level, value_weight, queries, key_states, spike_mask, out_grad):
    tok = hidden_in.shape[1]
    n_dp, n_seq = lax.axis_size("dp"), lax.axis_size("seq")
    assert 0 < WINDOW - 2 * tok <= tok and 2 * tok % BLOCK == 0

    def both(value):
        return value, swapped(value, "seq", 1)

    own_keys = key_states[0]
    query_own, query_out, grad_own, grad_out, marks_own, weight_half, key_tail = split(
        tok,
        queries[0],
        out_grad[0],
        jnp.transpose(spike_mask, (2, 0, 1)),
        spike_level,
        value_weight,
        own_keys,
    )
    near_keys, far_keys = lax.optimization_barrier(
        (shifted(own_keys, 2), shifted_odd(key_tail, 4))
    )
    query_oth, grad_oth, marks_oth = (
        swapped(value, "seq", 1) for value in (query_out, grad_out, marks_own)
    )
    near_keys, far_keys, query_oth, grad_oth, marks_oth = lax.optimization_barrier(
        (near_keys, far_keys, query_oth, grad_oth, marks_oth)
    )
    keys_own, keys_out = pack(tok, own_keys, near_keys, far_keys)
    if n_dp == 2:
        weight = (weight_half, swapped(weight_half, "dp", 1))
    else:
        weight = (lax.all_gather(weight_half, "dp", axis=0, tiled=True),)
    keys_oth, hidden_own, *weight = lax.optimization_barrier(
        (swapped(keys_out, "seq", 1), hidden_in[0], *weight)
    )
    raw = [query_own, query_oth, grad_own, grad_oth, keys_own, keys_oth]
    marks = (marks_own, marks_oth)

    own, near, far, top, norm, *heads = value_terms(tok, raw, marks)
    near, far = shifted(near, -2), shifted(far, -4)
    values, tail, spiked = project(tok, both(hidden_own), marks, weight)

    fast = n_dp == 2 and n_seq == 16 and hidden_in.shape[2] % 256 == 0
    if fast:
        keep, send = weight_terms(tok, spiked, (own, near, far))
        values, tail, send = lax.optimization_barrier((values, tail, send))
        got = crossed(send, n_seq)
    window = (values, shifted(values, 2), shifted(tail, 4))
    own_k, near_k, far_k, query_mine, query_out = key_terms(tok, heads, top, norm, window)
    if fast:
        got, own_k = lax.optimization_barrier((got, own_k))
        keep, *sends = reduce_step(keep, [got], 4)
        near_k, far_k, *sends = lax.optimization_barrier((near_k, far_k, *sends))
        got = [crossed(send, flip) for send, flip in zip(sends, (4, 2, 6))]
    near_k, far_k = shifted(near_k, -2), shifted(far_k, -4)
    if fast:
        (part,) = reduce_step(keep, got, 1)
        query_out, part = lax.optimization_barrier((query_out, part))
        got = crossed(part, 8)
    query_got = swapped(query_out, "seq", 1)
    if fast:
        got, near_k, far_k, query_got = lax.optimization_barrier((got, near_k, far_k, query_got))
        (owned,) = reduce_step(part, [got], 1, turned=True)
        near_k, owned = lax.optimization_barrier((near_k, owned))
    key_mine, key_out = sum_keys(tok, own_k, near_k, far_k)
    key_got = swapped(key_out, "seq", 1)
    query_grad, key_grad = place_tokens(query_mine, query_got, key_mine, key_got)
    if fast:
        pieces = [crossed(owned, flip) for flip in (4, 2, 6)]
        *pieces, key_grad = lax.optimization_barrier((*pieces, key_grad))
        pieces = [owned, *pieces]
        weight_grad = place_weight(*pieces, *[swapped(piece, "seq", 1) for piece in pieces])
    else:
        value_grad = value_sum(tok, own, near, far).astype(bf16)
        weight_grad = reduce_any(spiked, value_grad)
    return (query_grad[None], key_grad[None], weight_grad)


def solution(mesh):
    placed = (
        P("dp", "seq", None),
        P("dp", "seq"),
        P("dp", None),
        P("dp", "seq", None),
        P("dp", "seq", None),
        P("dp", "seq", None),
        P("dp", "seq", None),
    )
    return jax.shard_map(
        body,
        mesh=mesh,
        in_specs=placed,
        out_specs=(P("dp", "seq", None), P("dp", "seq", None), P("dp", None)),
        check_vma=False,
    )
```
